128 devices in a mesh: curve: 128 (over x, y, z, core).
Axes of the slice: x: 4, y: 4, z: 4, core: 2. Of those that a mesh axis runs over, the one named last changes fastest.
Arguments:
- fields: float32 [512, 6, 128, 128], P('curve'), as said below
- wet_mask: int32 [512, 128, 128], P('curve'), may hold values 0 or 1
- neighbors: int32 [512, 4], replicated, may hold values from -1 to 511, as said below
- migration: int32 [128, 1], replicated, may hold values from 0 to 3, as said below
Outputs:
- final_fields: float32 [512, 6, 128, 128], P('curve')
The draws below stay inside these ranges and needn't reach their ends.
Inputs may be any that keep to these rules, and one draw needn't show every extreme that they name: `fields`: field 0 (depth) is 0.3 or more before masking, field 5 lies between 0.01 and 0.1. The patches form a rectangular grid; row p names its west, east, south and north neighbors, -1 at the grid's boundary, and the relation is symmetric. Row d names 1 different slots of owner d; the patch in slot migration[d, k] moves to owner d + 1 (owner 0 after the last) and takes slot migration[d + 1, k] there.
All inputs are finite; a program needn't handle non-finite values. No bound on the sum of `wet_mask` on one device may be relied on, other than what follows from the above.
Results may differ from the reference program's by a relative error of at most 0.00002.
Values sent between devices are 32-bit elements; how exact they have to be, the bound alone decides.
No kernel may reach another device: no remote copies, remote signals or barrier semaphores. Data moves between devices by JAX's collectives and lax.ppermute only.
A program may use at most 128 MiB of HBM per device.

```python
import math
import jax
import jax.numpy as jnp
from jax import lax

PS = 128
P_DEV = 4
MIG = 1
OWNERS = 128
PATCHES = 512


def draw_fields(key, part):
    subkeys = jax.random.split(key, 6)
    extent = (PATCHES, PS, PS)
    water = 0.5 + 2.0 * jax.random.uniform(subkeys[0], extent)
    flow_x = water * 0.3 * jnp.clip(jax.random.normal(subkeys[1], extent), -3.0, 3.0)
    flow_y = water * 0.3 * jnp.clip(jax.random.normal(subkeys[2], extent), -3.0, 3.0)
    bed_level = 0.2 * jnp.clip(jax.random.normal(subkeys[4], extent), -3.0, 3.0)
    sediment = water * jax.random.uniform(subkeys[3], extent, minval=0.0, maxval=0.06)
    friction = jnp.exp(jax.random.uniform(subkeys[5], extent, minval=math.log(0.01), maxval=math.log(0.1)))
    return jnp.stack([water, flow_x, flow_y, sediment, bed_level, friction], 1).astype(jnp.float32)


def draw_neighbors(key, part):
    patch_count = PATCHES
    bit_count = patch_count.bit_length() - 1
    across_bits = (bit_count + 1) // 2
    upward_bits = bit_count - across_bits
    grid_across = 1 << across_bits
    grid_upward = 1 << upward_bits
    subkeys = jax.random.split(key, 2)
    lower_pattern = jnp.array([0] * (across_bits - 1) + [1] * upward_bits, dtype=jnp.int32)
    ordering = jnp.concatenate([jax.random.permutation(subkeys[0], lower_pattern), jnp.zeros((1,), jnp.int32)])
    is_across = (ordering == 0).astype(jnp.int32)
    across_rank = jnp.cumsum(is_across) - is_across
    upward_rank = jnp.cumsum(1 - is_across) - (1 - is_across)
    curve_index = jnp.arange(patch_count, dtype=jnp.int32)
    column = jnp.zeros(patch_count, jnp.int32)
    row_place = jnp.zeros(patch_count, jnp.int32)
    for level in range(bit_count):
        digit = jnp.right_shift(curve_index, level) & 1
        column = column + jnp.where(ordering[level] == 0, jnp.left_shift(digit, across_rank[level]), 0)
        row_place = row_place + jnp.where(ordering[level] == 1, jnp.left_shift(digit, upward_rank[level]), 0)
    top_digit = jnp.right_shift(curve_index, bit_count - 1) & 1
    column = jnp.where(top_digit == 1, jnp.bitwise_xor(column, grid_across // 2 - 1), column)
    flipping = jax.random.randint(subkeys[1], (2,), 0, 2)
    column = jnp.where(flipping[0] == 1, grid_across - 1 - column, column)
    row_place = jnp.where(flipping[1] == 1, grid_upward - 1 - row_place, row_place)
    position = row_place * grid_across + column
    lookup = jnp.zeros(patch_count, jnp.int32).at[position].set(curve_index)
    west = jnp.where(column > 0, lookup[jnp.maximum(position - 1, 0)], -1)
    east = jnp.where(column < grid_across - 1, lookup[jnp.minimum(position + 1, patch_count - 1)], -1)
    south = jnp.where(row_place > 0, lookup[jnp.maximum(position - grid_across, 0)], -1)
    north = jnp.where(row_place < grid_upward - 1, lookup[jnp.minimum(position + grid_across, patch_count - 1)], -1)
    return jnp.stack([west, east, south, north], 1).astype(jnp.int32)


def draw_migration(key, part):
    scores = jax.random.randint(key, (OWNERS, P_DEV), 0, 1 << 20) * P_DEV + jnp.arange(P_DEV, dtype=jnp.int32)[None, :]
    ordering = jnp.argsort(scores, axis=1)
    return ordering[:, :MIG].astype(jnp.int32)


def with_ends(values, rng, low, largest):
    shape = values.shape
    spot = [jax.random.randint(jax.random.fold_in(rng, axis), (), 0, shape[axis]) for axis in range(len(shape))]
    values = values.at[tuple(spot)].set(low)
    longest = shape.index(max(shape))
    spot[longest] = (spot[longest] + 1) % shape[longest]
    return values.at[tuple(spot)].set(largest)


def setup_inputs(seed: int = 0) -> dict:
    splits = jax.random.split(jax.random.key(seed), 5)
    fields = draw_fields(jax.random.fold_in(splits[4], 71), 0)
    wet_mask = with_ends((jax.random.randint(splits[1], (PATCHES, PS, PS), 0, 4) < 3).astype(jnp.int32), jax.random.fold_in(splits[1], 1), 0, 1)
    neighbors = draw_neighbors(jax.random.fold_in(splits[4], 71), 0)
    migration = draw_migration(jax.random.fold_in(splits[4], 71), 0)
    return dict(fields=fields, wet_mask=wet_mask, neighbors=neighbors, migration=migration)


GRAVITY = 9.81
TIME_STEP = 0.04
DRY_EPS = 0.01
CAPACITY = 0.02
EROSION = 0.5
SETTLING = 0.2
POROSITY = 0.4

def face_flux(left_depth, left_normal, left_along, left_sed, right_depth, right_normal, right_along, right_sed):
    left_inverse = left_depth / (left_depth * left_depth + DRY_EPS)
    right_inverse = right_depth / (right_depth * right_depth + DRY_EPS)
    left_speed = left_normal * left_inverse
    right_speed = right_normal * right_inverse
    left_cross = left_along * left_inverse
    right_cross = right_along * right_inverse
    left_conc = left_sed * left_inverse
    right_conc = right_sed * right_inverse
    left_root = jnp.sqrt(jnp.maximum(left_depth, 0.0) + 0.01)
    right_root = jnp.sqrt(jnp.maximum(right_depth, 0.0) + 0.01)
    weights = left_root + right_root
    mean_speed = (left_root * left_speed + right_root * right_speed) / weights
    mean_cross = (left_root * left_cross + right_root * right_cross) / weights
    mean_conc = (left_root * left_conc + right_root * right_conc) / weights
    celerity = jnp.sqrt(GRAVITY * 0.5 * (jnp.maximum(left_depth, 0.0) + jnp.maximum(right_depth, 0.0))) + 0.1
    jump_depth = right_depth - left_depth
    jump_normal = right_normal - left_normal
    jump_along = right_along - left_along
    jump_sed = right_sed - left_sed
    slow_wave = ((mean_speed + celerity) * jump_depth - jump_normal) / (2.0 * celerity)
    fast_wave = (jump_normal - (mean_speed - celerity) * jump_depth) / (2.0 * celerity)
    shear_wave = jump_along - mean_cross * jump_depth
    sed_wave = jump_sed - mean_conc * jump_depth
    slow_part = jnp.abs(mean_speed - celerity) * slow_wave
    fast_part = jnp.abs(mean_speed + celerity) * fast_wave
    middle = jnp.abs(mean_speed)
    both_parts = slow_part + fast_part
    flux_depth = 0.5 * (left_normal + right_normal) - 0.5 * both_parts
    flux_normal = 0.5 * (left_normal * left_speed + 0.5 * GRAVITY * left_depth * left_depth + right_normal * right_speed + 0.5 * GRAVITY * right_depth * right_depth) - 0.5 * (slow_part * (mean_speed - celerity) + fast_part * (mean_speed + celerity))
    flux_along = 0.5 * (left_normal * left_cross + right_normal * right_cross) - 0.5 * (both_parts * mean_cross + middle * shear_wave)
    flux_sed = 0.5 * (left_normal * left_conc + right_normal * right_conc) - 0.5 * (both_parts * mean_conc + middle * sed_wave)
    return (flux_depth, flux_normal, flux_along, flux_sed)

def inner_part(field):
    return field[..., 1:-1, 1:-1]

def x_change(flux):
    return flux[..., 1:] - flux[..., :-1]

def y_change(flux):
    return flux[..., 1:, :] - flux[..., :-1, :]

def advance(extended):
    water = extended[..., 0, :, :]
    flow_x = extended[..., 1, :, :]
    flow_y = extended[..., 2, :, :]
    sediment = extended[..., 3, :, :]
    bed_level = extended[..., 4, :, :]
    friction = extended[..., 5, :, :]
    x_flux = face_flux(water[..., 1:-1, :-1], flow_x[..., 1:-1, :-1], flow_y[..., 1:-1, :-1], sediment[..., 1:-1, :-1], water[..., 1:-1, 1:], flow_x[..., 1:-1, 1:], flow_y[..., 1:-1, 1:], sediment[..., 1:-1, 1:])
    y_flux = face_flux(water[..., :-1, 1:-1], flow_y[..., :-1, 1:-1], flow_x[..., :-1, 1:-1], sediment[..., :-1, 1:-1], water[..., 1:, 1:-1], flow_y[..., 1:, 1:-1], flow_x[..., 1:, 1:-1], sediment[..., 1:, 1:-1])
    old_water = inner_part(water)
    new_water = old_water - TIME_STEP * (x_change(x_flux[0]) + y_change(y_flux[0]))
    new_x = inner_part(flow_x) - TIME_STEP * (x_change(x_flux[1]) + y_change(y_flux[2])) - TIME_STEP * GRAVITY * old_water * 0.5 * (bed_level[..., 1:-1, 2:] - bed_level[..., 1:-1, :-2])
    new_y = inner_part(flow_y) - TIME_STEP * (x_change(x_flux[2]) + y_change(y_flux[1])) - TIME_STEP * GRAVITY * old_water * 0.5 * (bed_level[..., 2:, 1:-1] - bed_level[..., :-2, 1:-1])
    new_sed = inner_part(sediment) - TIME_STEP * (x_change(x_flux[3]) + y_change(y_flux[3]))
    inverse = new_water / (new_water * new_water + DRY_EPS)
    speed = jnp.sqrt((new_x * inverse) ** 2 + (new_y * inverse) ** 2)
    inner_friction = inner_part(friction)
    factor = 1.0 / (1.0 + TIME_STEP * inner_friction * speed / (jnp.maximum(new_water, 0.0) + 0.1))
    new_x = new_x * factor
    new_y = new_y * factor
    concentration = new_sed * inverse
    net_rate = EROSION * jnp.maximum(CAPACITY * speed * speed - concentration, 0.0) - SETTLING * concentration
    new_sed = new_sed + TIME_STEP * net_rate
    new_bed = inner_part(bed_level) - TIME_STEP * net_rate / (1.0 - POROSITY)
    return jnp.stack([new_water, new_x, new_y, new_sed, new_bed, inner_friction], -3)

def pick_from(source, which, fallback):
    usable = (which >= 0)[:, None, None, None]
    return jnp.where(usable, source[jnp.maximum(which, 0)], fallback)

def extend(patches, neighbors):
    extent = patches.shape[-1]
    west = pick_from(patches[..., extent - 2:], neighbors[:, 0], jnp.repeat(patches[..., :1], 2, -1))
    east = pick_from(patches[..., :2], neighbors[:, 1], jnp.repeat(patches[..., -1:], 2, -1))
    widened = jnp.concatenate([west, patches, east], -1)
    south = pick_from(widened[..., extent - 2:extent, :], neighbors[:, 2], jnp.repeat(widened[..., :1, :], 2, -2))
    north = pick_from(widened[..., :2, :], neighbors[:, 3], jnp.repeat(widened[..., -1:, :], 2, -2))
    return jnp.concatenate([south, widened, north], -2)

def two_steps(patch_block):
    return advance(advance(patch_block))

def run_round(patches, neighbors):
    extended = extend(patches, neighbors)
    side = extended.shape[-1]
    blocks = extended.reshape(-1, P_DEV, 6, side, side)
    stepped = lax.map(two_steps, blocks)
    return stepped.reshape(-1, 6, side - 4, side - 4)

def reference(fields, wet_mask, neighbors, migration):
    wetness = wet_mask.astype(jnp.float32)
    unity = jnp.ones_like(wetness)
    scaling = jnp.stack([wetness, wetness, wetness, wetness, unity, unity], 1)
    patches = fields * scaling
    patches = run_round(patches, neighbors)
    patches = run_round(patches, neighbors)
    owner_count = migration.shape[0]
    layout = jnp.arange(owner_count * P_DEV, dtype=jnp.int32).reshape(owner_count, P_DEV)
    previous = (jnp.arange(owner_count, dtype=jnp.int32) - 1) % owner_count
    incoming = previous[:, None] * P_DEV + jnp.roll(migration, 1, axis=0)
    layout = layout.at[jnp.arange(owner_count, dtype=jnp.int32)[:, None], migration].set(incoming)
    return patches[layout.reshape(-1)]
```

```python
import jax
import jax.numpy as jnp
from jax import lax
from jax.experimental import pallas as pl
from jax.experimental.pallas import tpu as pltpu
from jax.sharding import PartitionSpec as P

GRAVITY = 9.81
TIME_STEP = 0.04
DRY_EPS = 0.01
CAPACITY = 0.02
EROSION = 0.5
SETTLING = 0.2
POROSITY = 0.4

F32 = jnp.float32
NF = 6
N = 128
SUB = 8
JM = 16
JC = 17
KR = 12
VMEM_LIMIT = 24 * 1024 * 1024

NORTH, SOUTH, NORTH_CORNER, SOUTH_CORNER = 48, 71, 94, 111


def lanes_of(shape):
    return lax.broadcasted_iota(jnp.int32, shape, 1)


def subs_of(shape):
    return lax.broadcasted_iota(jnp.int32, shape, 0)


def lane_roll(v, shift):
    return pltpu.roll(v, shift % N, 1)


def cell_terms(h, qx, qy, m):
    hp = jnp.maximum(h, 0.0)
    a = h / (h * h + DRY_EPS)
    u, v, s = qx * a, qy * a, m * a
    r = jnp.sqrt(hp + 0.01)
    half = (0.5 * GRAVITY) * h * h
    return dict(
        h=h, hp=hp, qx=qx, qy=qy, m=m, r=r, ru=r * u, rv=r * v, rs=r * s,
        fxx=qx * u + half, fxy=qx * v, fyy=qy * v + half, fxs=qx * s, fys=qy * s,
    )


ROLLED_X = ("h", "qx", "qy", "m", "r", "ru", "rv", "rs", "fxx", "fxy", "fxs")


def face_twice(L, R, along_x):
    qn, qt, rn, rt, fn, fs = (
        ("qx", "qy", "ru", "rv", "fxx", "fxs") if along_x else ("qy", "qx", "rv", "ru", "fyy", "fys")
    )
    w = L["r"] + R["r"]
    c2 = jnp.sqrt((2.0 * GRAVITY) * (L["hp"] + R["hp"])) + 0.2
    c = 0.5 * c2
    inv = 1.0 / (w * c2)
    iw, ic2 = inv * c2, inv * w
    U = (L[rn] + R[rn]) * iw
    W = (L[rt] + R[rt]) * iw
    S = (L["rs"] + R["rs"]) * iw
    dh = R["h"] - L["h"]
    dn = R[qn] - L[qn]
    dt = R[qt] - L[qt]
    dm = R["m"] - L["m"]
    up, um = U + c, U - c
    p1 = jnp.abs(um) * ((up * dh - dn) * ic2)
    p3 = jnp.abs(up) * ((dn - um * dh) * ic2)
    mid = jnp.abs(U)
    b = p1 + p3
    f_h = (L[qn] + R[qn]) - b
    f_n = (L[fn] + R[fn]) - (p1 * um + p3 * up)
    f_t = (L["fxy"] + R["fxy"]) - (b * W + mid * (dt - W * dh))
    f_s = (L[fs] + R[fs]) - (b * S + mid * (dm - S * dh))
    return f_h, f_n, f_t, f_s


def update(C, bed, bed_e, bed_w, bed_n, bed_s, fric, fxe, fxw, fyn, fys):
    k = 0.5 * TIME_STEP
    h = C["h"]
    slope = (TIME_STEP * GRAVITY * 0.5) * h
    nh = h - k * ((fxe[0] - fxw[0]) + (fyn[0] - fys[0]))
    nx = C["qx"] - k * ((fxe[1] - fxw[1]) + (fyn[2] - fys[2])) - slope * (bed_e - bed_w)
    ny = C["qy"] - k * ((fxe[2] - fxw[2]) + (fyn[1] - fys[1])) - slope * (bed_n - bed_s)
    nm = C["m"] - k * ((fxe[3] - fxw[3]) + (fyn[3] - fys[3]))
    a = nh / (nh * nh + DRY_EPS)
    vx, vy = nx * a, ny * a
    speed2 = vx * vx + vy * vy
    speed = jnp.sqrt(speed2)
    depth = jnp.maximum(nh, 0.0) + 0.1
    factor = depth / (depth + (TIME_STEP * fric) * speed)
    conc = nm * a
    net = EROSION * jnp.maximum(CAPACITY * speed2 - conc, 0.0) - SETTLING * conc
    nm = nm + TIME_STEP * net
    nb = bed - (TIME_STEP / (1.0 - POROSITY)) * net
    return nh, nx * factor, ny * factor, nm, nb


def advance_tiles(load, store, lo, hi, last):
    def raw(j, f):
        if j < 0:
            return pltpu.roll(load(last - 1, f), 1, 0)
        if j == last:
            return pltpu.roll(load(0, f), SUB - 1, 0)
        return load(j, f)

    def cell(j):
        return cell_terms(*(raw(j, f) for f in range(4)))

    cur = cell(lo)
    south = face_twice(cell(lo - 1), cur, False)
    for j in range(lo, hi):
        nxt = cell(j + 1)
        north = face_twice(cur, nxt, False)
        R = {key: lane_roll(cur[key], -1) for key in ROLLED_X}
        R["hp"] = jnp.maximum(R["h"], 0.0)
        east = face_twice(cur, R, True)
        west = tuple(lane_roll(x, 1) for x in east)
        bed = load(j, 4)
        new = update(
            cur, bed, lane_roll(bed, -1), lane_roll(bed, 1), raw(j + 1, 4), raw(j - 1, 4), load(j, 5),
            east, west, north, south,
        )
        for f in range(5):
            store(j, f, new[f])
        cur, south = nxt, north


def slot_of(i, moving):
    if i == 3:
        return moving
    return i + (moving <= i).astype(jnp.int32)


def message_kernel(mig_ref, fields_ref, mask_ref, out_ref, leave_ref, fbuf, mbuf, tbuf, fsem, msem):
    dev = lax.axis_index("curve")
    moving = mig_ref[0, dev]
    copies = []
    for t in range(4):
        a = pltpu.make_async_copy(fields_ref.at[t], fbuf.at[t], fsem.at[t])
        b = pltpu.make_async_copy(mask_ref.at[t], mbuf.at[t], msem.at[t])
        a.start()
        b.start()
        copies.append((a, b))
    lane = lanes_of((N, N))
    for t in range(4):
        for cp in copies[t]:
            cp.wait()
        wet = mbuf[t].astype(F32)
        for f in range(4):
            fbuf[t, f] = fbuf[t, f] * wet

        @pl.when(moving == t)
        def _():
            leave_ref[...] = fbuf[t]

        for f in range(NF):
            depth = 4 if f < 5 else 3
            low = 0 if f < 5 else 1
            tbuf[NORTH + 4 * f : NORTH + 4 * f + depth, :] = fbuf[t, f, 124 + low : 128, :]
            tbuf[SOUTH + 4 * f : SOUTH + 4 * f + depth, :] = fbuf[t, f, 0:depth, :]
            tbuf[NORTH_CORNER + 3 * f : NORTH_CORNER + 3 * f + depth - 1, :] = fbuf[t, f, 129 - depth + low : 128, :] if f < 5 else fbuf[t, f, 126:128, :]
            tbuf[SOUTH_CORNER + 3 * f : SOUTH_CORNER + 3 * f + depth - 1, :] = fbuf[t, f, 0 : depth - 1, :]
        acc = jnp.transpose(tbuf[...])
        for f in range(NF):
            v = fbuf[t, f]
            acc = jnp.where((lane >= 8 * f) & (lane < 8 * f + 4), lane_roll(v, 8 * f), acc)
            acc = jnp.where((lane >= 8 * f + 4) & (lane < 8 * f + 8), lane_roll(v, 8 * f + 8), acc)
        out_ref[pl.ds(t, N, stride=4), :] = acc


def make_messages(mig, fields, mask):
    return pl.pallas_call(
        message_kernel,
        out_shape=(
            jax.ShapeDtypeStruct((4 * N, N), F32),
            jax.ShapeDtypeStruct((NF, N, N), F32),
        ),
        in_specs=[
            pl.BlockSpec(memory_space=pltpu.SMEM),
            pl.BlockSpec(memory_space=pl.ANY),
            pl.BlockSpec(memory_space=pl.ANY),
        ],
        out_specs=(pl.BlockSpec(memory_space=pltpu.VMEM), pl.BlockSpec(memory_space=pltpu.VMEM)),
        scratch_shapes=[
            pltpu.VMEM((4, NF, N, N), F32),
            pltpu.VMEM((4, N, N), jnp.int32),
            pltpu.VMEM((N, N), F32),
            pltpu.SemaphoreType.DMA((4,)),
            pltpu.SemaphoreType.DMA((4,)),
        ],
        compiler_params=pltpu.CompilerParams(vmem_limit_bytes=VMEM_LIMIT),
        cost_estimate=pl.CostEstimate(flops=2_000_000, bytes_accessed=3_000_000, transcendentals=0),
        name="messages",
    )(mig, fields, mask)


def route_kernel(near_ref, mig_ref, rows_ref, out_ref):
    dev = lax.axis_index("curve")
    side = (dev < N // 2).astype(jnp.int32)
    lane = lanes_of((1, N))
    from_west = (lane < NORTH) & ((lane & 4) != 0)
    from_east = (lane < NORTH) & ((lane & 4) == 0)
    from_south = lane < SOUTH
    from_north = lane < NORTH_CORNER
    from_low = lane < SOUTH_CORNER

    def body(d, carry):
        moving = mig_ref[0, d]
        after = ((d + 1) & (N - 1)) * 4 + 3
        for t in range(4):
            p = 4 * d + t
            w = jnp.maximum(near_ref[0, p], 0)
            e = jnp.maximum(near_ref[1, p], 0)
            s = jnp.maximum(near_ref[2, p], 0)
            n = jnp.maximum(near_ref[3, p], 0)
            sc = jnp.maximum(near_ref[side, s], 0)
            nc = jnp.maximum(near_ref[side, n], 0)
            row = rows_ref[pl.ds(nc, 1), :]
            row = jnp.where(from_low, rows_ref[pl.ds(sc, 1), :], row)
            row = jnp.where(from_north, rows_ref[pl.ds(n, 1), :], row)
            row = jnp.where(from_south, rows_ref[pl.ds(s, 1), :], row)
            row = jnp.where(from_east, rows_ref[pl.ds(e, 1), :], row)
            row = jnp.where(from_west, rows_ref[pl.ds(w, 1), :], row)
            place = jnp.where(moving == t, after, p - (moving < t).astype(jnp.int32))
            out_ref[pl.ds(place, 1), :] = row
        return carry

    lax.fori_loop(0, N, body, 0, unroll=4)


def route(near, mig, rows):
    return pl.pallas_call(
        route_kernel,
        out_shape=jax.ShapeDtypeStruct((4 * N, N), F32),
        in_specs=[
            pl.BlockSpec(memory_space=pltpu.SMEM),
            pl.BlockSpec(memory_space=pltpu.SMEM),
            pl.BlockSpec(memory_space=pltpu.VMEM),
        ],
        out_specs=pl.BlockSpec(memory_space=pltpu.VMEM),
        compiler_params=pltpu.CompilerParams(vmem_limit_bytes=VMEM_LIMIT),
        cost_estimate=pl.CostEstimate(flops=2_000_000, bytes_accessed=2_000_000, transcendentals=0),
        name="route",
    )(near, mig, rows)


def own_strips(patch, i, lane, cols_ref, prev_ref, rows_ref):
    east = (lane >= 32 * i + 4) & (lane < 32 * i + 12)
    west = (lane >= 32 * i + 20) & (lane < 32 * i + 28)
    for f in range(NF):
        v = patch[f]
        old = prev_ref[f]
        old = jnp.where(east, lane_roll(v, 32 * i + 12), old)
        cols_ref[f] = jnp.where(west, lane_roll(v, 32 * i + 20), old)
        rows_ref[pl.ds((f * KR + 4) * SUB + 2 * i, 8, stride=SUB), :] = patch[f, 0:8, :]
        rows_ref[pl.ds((f * KR) * SUB + 2 * i + 1, 8, stride=SUB), :] = patch[f, 120:128, :]


def interior(patch, work, out_ref, which):
    for f in range(NF):
        for j in range(JM):
            work[0, f, j] = patch[f, pl.ds(j, SUB, stride=JM), :]
            if f == 5:
                work[1, f, j] = work[0, f, j]

    def step(k, carry):
        a, b = k & 1, 1 - (k & 1)

        def load(j, f):
            return work[a, f, j]

        def store(j, f, value):
            work[b, f, j] = value

        advance_tiles(load, store, 0, JM, JM)
        return carry

    lax.fori_loop(0, 4, step, 0)
    for f in range(NF):
        for j in range(JM):
            out_ref[which, f, pl.ds(j, SUB, stride=JM), :] = work[0, f, j]


def stay_kernel(mig_ref, fields_ref, mask_ref, out_ref, cols_ref, rows_ref, fbuf, mbuf, work, fsem, msem):
    count = out_ref.shape[0]
    moving = mig_ref[0, lax.axis_index("curve")]
    copies = []
    for i in range(count):
        slot = slot_of(i, moving)
        a = pltpu.make_async_copy(fields_ref.at[slot], fbuf.at[i], fsem.at[i])
        b = pltpu.make_async_copy(mask_ref.at[slot], mbuf.at[i], msem.at[i])
        a.start()
        b.start()
        copies.append((a, b))
    for f in range(NF):
        cols_ref[f] = jnp.zeros((N, N), F32)
    rows_ref[...] = jnp.zeros(rows_ref.shape, F32)
    lane = lanes_of((N, N))
    for i in range(count):
        for cp in copies[i]:
            cp.wait()
        wet = mbuf[i].astype(F32)
        for f in range(4):
            fbuf[i, f] = fbuf[i, f] * wet
        own_strips(fbuf.at[i], i, lane, cols_ref, cols_ref, rows_ref)

    def run(i, carry):
        interior(fbuf.at[i], work, out_ref, i)
        return carry

    lax.fori_loop(0, count, run, 0)


def stay(mig, fields, mask, count):
    return pl.pallas_call(
        stay_kernel,
        out_shape=(
            jax.ShapeDtypeStruct((count, NF, N, N), F32),
            jax.ShapeDtypeStruct((NF, N, N), F32),
            jax.ShapeDtypeStruct((NF * KR * SUB, N), F32),
        ),
        in_specs=[
            pl.BlockSpec(memory_space=pltpu.SMEM),
            pl.BlockSpec(memory_space=pl.ANY),
            pl.BlockSpec(memory_space=pl.ANY),
        ],
        out_specs=tuple(pl.BlockSpec(memory_space=pltpu.VMEM) for _ in range(3)),
        scratch_shapes=[
            pltpu.VMEM((count, NF, N, N), F32),
            pltpu.VMEM((count, N, N), jnp.int32),
            pltpu.VMEM((2, NF, JM, SUB, N), F32),
            pltpu.SemaphoreType.DMA((count,)),
            pltpu.SemaphoreType.DMA((count,)),
        ],
        compiler_params=pltpu.CompilerParams(vmem_limit_bytes=VMEM_LIMIT),
        cost_estimate=pl.CostEstimate(flops=30_000_000 * count, bytes_accessed=800_000 * count, transcendentals=0),
        name="stay",
    )(mig, fields, mask)


def arrive_kernel(patch_ref, cols_in, rows_in, out_ref, cols_ref, rows_ref, work):
    lane = lanes_of((N, N))
    rows_ref[...] = rows_in[...]
    own_strips(patch_ref, 3, lane, cols_ref, cols_in, rows_ref)
    interior(patch_ref, work, out_ref, 0)


def arrive(patch, cols, rows):
    return pl.pallas_call(
        arrive_kernel,
        out_shape=(
            jax.ShapeDtypeStruct((1, NF, N, N), F32),
            jax.ShapeDtypeStruct((NF, N, N), F32),
            jax.ShapeDtypeStruct((NF * KR * SUB, N), F32),
        ),
        in_specs=[pl.BlockSpec(memory_space=pltpu.VMEM)] * 3,
        out_specs=tuple(pl.BlockSpec(memory_space=pltpu.VMEM) for _ in range(3)),
        scratch_shapes=[pltpu.VMEM((2, NF, JM, SUB, N), F32)],
        compiler_params=pltpu.CompilerParams(vmem_limit_bytes=VMEM_LIMIT),
        cost_estimate=pl.CostEstimate(flops=30_000_000, bytes_accessed=800_000, transcendentals=0),
        name="arrive",
    )(patch, cols, rows)


def finish_kernel(
    near_ref, mig_ref, halo_ref, cols_ref, rows_ref, stay_ref, come_ref, out_ref,
    wide, flip, cwork, rwork, stage, sem,
):
    dev = lax.axis_index("curve")
    moving = mig_ref[0, dev]
    before = (dev + N - 1) & (N - 1)
    lane = lanes_of((SUB, N))
    sub = subs_of((SUB, N))
    group = lane // 32

    lacks = []
    for i in range(4):
        patch = 4 * dev + slot_of(i, moving) if i < 3 else 4 * before + mig_ref[0, before]
        lacks.append([(near_ref[k, patch] < 0).astype(jnp.int32) for k in range(4)])

    def by_group(k):
        v = jnp.zeros((SUB, N), jnp.int32)
        for i in range(4):
            v = jnp.where(group == i, lacks[i][k], v)
        return v != 0

    in_group = lane & 31
    no_west, no_east, no_south, no_north = (by_group(k) for k in range(4))
    west1, west2 = no_west & (in_group == 19), no_west & (in_group == 18)
    east1, east2 = no_east & (in_group == 12), no_east & (in_group == 13)
    low_fix = no_south & (sub == 0)
    high_fix = no_north & (sub == 7)
    row_flag = jnp.zeros((SUB, N), jnp.int32)
    for i in range(4):
        row_flag = jnp.where(sub == 2 * i, lacks[i][2], row_flag)
        row_flag = jnp.where(sub == 2 * i + 1, lacks[i][3], row_flag)
    row_low = (row_flag != 0) & ((sub & 1) == 0)
    row_high = (row_flag != 0) & ((sub & 1) == 1)

    lane_all = lanes_of((N, N))
    for f in range(NF):
        acc = cols_ref[f]
        for i in range(4):
            inside = (lane_all >= 32 * i + 12) & (lane_all < 32 * i + 20)
            acc = jnp.where(inside, lane_roll(halo_ref[pl.ds(i, N, stride=4), :], 32 * i + 12 - 8 * f), acc)
        wide[f, 4 : 4 + N, :] = acc
        rwork[0, f] = rows_ref[f * KR : (f + 1) * KR]
        rwork[1, f] = rows_ref[f * KR : (f + 1) * KR]
    lane4 = lanes_of((4, N))
    for i in range(4):
        flip[0:N, :] = jnp.transpose(halo_ref[pl.ds(i, N, stride=4), :])
        for f in range(NF):
            for high in range(2):
                if high:
                    edge = flip[SOUTH + 4 * f : SOUTH + 4 * f + 4, :]
                    corner = flip[SOUTH_CORNER + 3 * f : SOUTH_CORNER + 3 * f + 4, :]
                else:
                    shift = 0 if f < 5 else 1
                    edge = flip[NORTH + 4 * f - shift : NORTH + 4 * f - shift + 4, :]
                    first = NORTH_CORNER - 1 + 3 * f if f < 5 else NORTH_CORNER + 13
                    corner = flip[first : first + 4, :]
                low_half = lane4 < N // 2
                a = lane_roll(jnp.where(low_half, corner, edge), 32 * i + 12)
                b = lane_roll(jnp.where(low_half, edge, corner), 32 * i + 20)
                ends = jnp.where((lane4 & 31) < 16, a, b)
                at = 132 if high else 0
                if i == 0:
                    wide[f, at : at + 4, :] = ends
                else:
                    wide[f, at : at + 4, :] = jnp.where(lane4 // 32 == i, ends, wide[f, at : at + 4, :])
                k0 = 8 if high else 0
                for r in range(4):
                    rwork[0, f, k0 + r, 2 * i + high : 2 * i + high + 1, :] = edge[r : r + 1, :]
                    if f == 5:
                        rwork[1, f, k0 + r, 2 * i + high : 2 * i + high + 1, :] = edge[r : r + 1, :]
    for f in range(NF):
        for j in range(JC):
            cwork[0, f, j] = wide[f, pl.ds(j, SUB, stride=JC), :]

    def edges(fields):
        for f in fields:
            for j in range(JC):
                v = cwork[0, f, j]
                v = jnp.where(
                    west1, lane_roll(v, -1), jnp.where(west2, lane_roll(v, -2), v)
                )
                v = jnp.where(
                    east1, lane_roll(v, 1), jnp.where(east2, lane_roll(v, 2), v)
                )
                cwork[0, f, j] = v
            for j in (2, 3):
                cwork[0, f, j] = jnp.where(low_fix, cwork[0, f, 4], cwork[0, f, j])
            for j in (13, 14):
                cwork[0, f, j] = jnp.where(high_fix, cwork[0, f, 12], cwork[0, f, j])
            for k in (2, 3):
                rwork[0, f, k] = jnp.where(row_low, rwork[0, f, 4], rwork[0, f, k])
            for k in (8, 9):
                rwork[0, f, k] = jnp.where(row_high, rwork[0, f, 7], rwork[0, f, k])

    edges((5,))
    for j in range(JC):
        cwork[1, 5, j] = cwork[0, 5, j]
    for k in range(KR):
        rwork[1, 5, k] = rwork[0, 5, k]

    def half_step(a, b, lo, hi):
        def loader(ref):
            return lambda j, f: ref[a, f, j]

        def storer(ref):
            def put(j, f, value):
                ref[b, f, j] = value

            return put

        advance_tiles(loader(cwork), storer(cwork), 0, JC, JC)
        advance_tiles(loader(rwork), storer(rwork), lo, hi, KR)

    def both(r, carry):
        edges(range(5))
        half_step(0, 1, 1, KR - 1)
        half_step(1, 0, 2, KR - 2)
        return carry

    lax.fori_loop(0, 2, both, 0)

    for f in range(NF):
        for j in range(JC):
            wide[f, pl.ds(j, SUB, stride=JC), :] = cwork[0, f, j]
    copies = []
    for i in range(4):
        src = stay_ref.at[i] if i < stay_ref.shape[0] else come_ref.at[i - stay_ref.shape[0]]
        for f in range(NF):
            strip = wide[f, 4 : 4 + N, :]
            v = src[f]
            stage[i, f] = v
            for r in range(4):
                stage[i, f, r : r + 1, :] = rwork[0, f, 4 + r, 2 * i : 2 * i + 1, :]
                stage[i, f, 124 + r : 125 + r, :] = rwork[0, f, 4 + r, 2 * i + 1 : 2 * i + 2, :]
            v = stage[i, f]
            v = jnp.where(lane_all < 4, lane_roll(strip, 108 - 32 * i), v)
            stage[i, f] = jnp.where(lane_all >= 124, lane_roll(strip, 116 - 32 * i), v)
        cp = pltpu.make_async_copy(stage.at[i], out_ref.at[slot_of(i, moving)], sem.at[i])
        cp.start()
        copies.append(cp)
    for cp in copies:
        cp.wait()


def finish(near, mig, halo, cols, rows, stayed, came):
    smem, vmem = pl.BlockSpec(memory_space=pltpu.SMEM), pl.BlockSpec(memory_space=pltpu.VMEM)
    return pl.pallas_call(
        finish_kernel,
        out_shape=jax.ShapeDtypeStruct((4, NF, N, N), F32),
        in_specs=[smem, smem, vmem, vmem, vmem, vmem, vmem],
        out_specs=pl.BlockSpec(memory_space=pl.ANY),
        scratch_shapes=[
            pltpu.VMEM((NF, 136, N), F32),
            pltpu.VMEM((136, N), F32),
            pltpu.VMEM((2, NF, JC, SUB, N), F32),
            pltpu.VMEM((2, NF, KR, SUB, N), F32),
            pltpu.VMEM((4, NF, N, N), F32),
            pltpu.SemaphoreType.DMA((4,)),
        ],
        compiler_params=pltpu.CompilerParams(vmem_limit_bytes=VMEM_LIMIT),
        cost_estimate=pl.CostEstimate(flops=30_000_000, bytes_accessed=3_000_000, transcendentals=0),
        name="finish",
    )(near, mig, halo, cols, rows, stayed, came)


def swap(rows):
    return lax.all_to_all(rows.reshape(N, 4, N), "curve", 0, 0, tiled=True).reshape(4 * N, N)


def shards(fields, wet_mask, neighbors, migration):
    near, mig = neighbors.T, migration.T
    owners = lax.axis_size("curve")
    messages, leaving = make_messages(mig, fields, wet_mask)
    spread = swap(messages)
    patch = lax.ppermute(leaving, "curve", [(d, (d + 1) % owners) for d in range(owners)])
    stayed, cols, rows = stay(mig, fields, wet_mask, 3)
    halo = swap(route(near, mig, spread))
    came, cols, rows = arrive(patch, cols, rows)
    return finish(near, mig, halo, cols, rows.reshape(NF * KR, SUB, N), stayed, came)


def solution(mesh):
    placed = (P("curve", None, None, None), P("curve", None, None), P(), P())
    return jax.shard_map(
        shards, mesh=mesh, in_specs=placed, out_specs=P("curve", None, None, None), check_vma=False
    )
```

```python
import jax
import jax.numpy as jnp
from jax import lax
from jax.experimental import pallas as pl
from jax.experimental.pallas import tpu as pltpu
from jax.sharding import PartitionSpec as P

GRAVITY = 9.81
TIME_STEP = 0.04
DRY_EPS = 0.01
CAPACITY = 0.02
EROSION = 0.5
SETTLING = 0.2
POROSITY = 0.4

F32 = jnp.float32
NF = 6
N = 128
SUB = 8
JM = 16
JC = 17
KR = 12
VMEM_ALL = 67_043_328

NORTH, SOUTH, NORTH_CORNER, SOUTH_CORNER = 48, 71, 94, 111


def lanes_of(shape):
    return lax.broadcasted_iota(jnp.int32, shape, 1)


def subs_of(shape):
    return lax.broadcasted_iota(jnp.int32, shape, 0)


def lane_roll(v, shift):
    return pltpu.roll(v, shift % N, 1)


def root(x):
    return x * lax.rsqrt(x)


def root_from_zero(x):
    return root(jnp.maximum(x, 1e-30))


def cell_terms(h, qx, qy, m):
    hp = jnp.maximum(h, 0.0)
    h2 = h * h
    a = h / (h2 + DRY_EPS)
    u, v, s = qx * a, qy * a, m * a
    r = root(hp + 0.01)
    half = (0.5 * GRAVITY) * h2
    return dict(
        h=h, hp=hp, qx=qx, qy=qy, m=m, r=r, ru=r * u, rv=r * v, rs=r * s,
        fxx=qx * u + half, fxy=qx * v, fyy=qy * v + half, fxs=qx * s, fys=qy * s,
    )


ROLLED_X = ("h", "qx", "qy", "m", "r", "ru", "rv", "rs", "fxx", "fxy", "fxs")


def face_twice(L, R, along_x):
    qn, qt, rn, rt, fn, fs = (
        ("qx", "qy", "ru", "rv", "fxx", "fxs") if along_x else ("qy", "qx", "rv", "ru", "fyy", "fys")
    )
    c = root_from_zero((0.5 * GRAVITY) * (L["hp"] + R["hp"])) + 0.1
    iw, ic2 = 1.0 / (L["r"] + R["r"]), 1.0 / (c + c)
    U = (L[rn] + R[rn]) * iw
    W = (L[rt] + R[rt]) * iw
    S = (L["rs"] + R["rs"]) * iw
    dh = R["h"] - L["h"]
    dn = R[qn] - L[qn]
    dt = R[qt] - L[qt]
    dm = R["m"] - L["m"]
    up, um = U + c, U - c
    p1 = jnp.abs(um) * ((up * dh - dn) * ic2)
    p3 = jnp.abs(up) * ((dn - um * dh) * ic2)
    mid = jnp.abs(U)
    b = p1 + p3
    f_h = (L[qn] + R[qn]) - b
    f_n = (L[fn] + R[fn]) - (p1 * um + p3 * up)
    e = b - mid * dh
    f_t = (L["fxy"] + R["fxy"]) - (W * e + mid * dt)
    f_s = (L[fs] + R[fs]) - (S * e + mid * dm)
    return f_h, f_n, f_t, f_s


def update(C, bed, bed_e, bed_w, bed_n, bed_s, fric, dx, fyn, fys):
    k = 0.5 * TIME_STEP
    h = C["h"]
    slope = (TIME_STEP * GRAVITY * 0.5) * h
    nh = h - k * (dx[0] + (fyn[0] - fys[0]))
    nx = C["qx"] - k * (dx[1] + (fyn[2] - fys[2])) - slope * (bed_e - bed_w)
    ny = C["qy"] - k * (dx[2] + (fyn[1] - fys[1])) - slope * (bed_n - bed_s)
    nm = C["m"] - k * (dx[3] + (fyn[3] - fys[3]))
    a = nh / (nh * nh + DRY_EPS)
    vx, vy = nx * a, ny * a
    speed2 = vx * vx + vy * vy
    speed = root_from_zero(speed2)
    depth = jnp.maximum(nh, 0.0) + 0.1
    factor = depth / (depth + (TIME_STEP * fric) * speed)
    conc = nm * a
    net = EROSION * jnp.maximum(CAPACITY * speed2 - conc, 0.0) - SETTLING * conc
    nm = nm + TIME_STEP * net
    nb = bed - (TIME_STEP / (1.0 - POROSITY)) * net
    return nh, nx * factor, ny * factor, nm, nb


KEPT = ("r", "ru", "rv", "rs", "fxy", "fyy", "fys")
TERMS = len(KEPT) + 4


def x_pass(load, terms, j, faces):
    cur = cell_terms(*(load(j, f) for f in range(4)))
    for n, key in enumerate(KEPT):
        terms[n, j] = cur[key]
    if faces:
        R = {key: lane_roll(cur[key], -1) for key in ROLLED_X}
        R["hp"] = jnp.maximum(R["h"], 0.0)
        east = face_twice(cur, R, True)
        for n in range(4):
            terms[len(KEPT) + n, j] = east[n] - lane_roll(east[n], 1)


def y_pass(load, store, terms, lo, hi, last):
    wraps = lo == 0

    def around(j, get):
        if j < 0:
            return pltpu.roll(get(last - 1), 1, 0)
        if j == last:
            return pltpu.roll(get(0), SUB - 1, 0)
        return get(j)

    def cell(j):
        C = {key: around(j, lambda t: load(t, f)) for f, key in enumerate(("h", "qx", "qy", "m"))}
        for n, key in enumerate(KEPT):
            C[key] = around(j, lambda t: terms[n, t])
        C["hp"] = jnp.maximum(C["h"], 0.0)
        return C

    if wraps:
        top = face_twice(cell(last - 1), cell(last), False)
        south = tuple(pltpu.roll(x, 1, 0) for x in top)
    else:
        south = face_twice(cell(lo - 1), cell(lo), False)
    cur = cell(lo)
    for j in range(lo, hi):
        if wraps and j == last - 1:
            nxt, north = None, top
        else:
            nxt = cell(j + 1)
            north = face_twice(cur, nxt, False)
        bed = load(j, 4)
        dx = tuple(terms[len(KEPT) + n, j] for n in range(4))
        bed_n, bed_s = (around(t, lambda t: load(t, 4)) for t in (j + 1, j - 1))
        new = update(
            cur, bed, lane_roll(bed, -1), lane_roll(bed, 1), bed_n, bed_s, load(j, 5), dx, north, south,
        )
        for f in range(5):
            store(j, f, new[f])
        cur, south = nxt, north


def advance_tiles(load, store, terms, lo, hi, last):
    span = range(last) if lo == 0 else range(lo - 1, hi + 1)
    for j in span:
        x_pass(load, terms, j, lo <= j < hi)
    y_pass(load, store, terms, lo, hi, last)


def slot_of(i, moving):
    if i == 3:
        return moving
    return i + (moving <= i).astype(jnp.int32)


def message_kernel(mig_hbm, fields_ref, mask_ref, out_ref, leave_ref, fbuf, mbuf, tbuf, mig_ref, fsem, msem, gsem, lsem):
    def fetches(t):
        return (
            pltpu.make_async_copy(fields_ref.at[t], fbuf.at[t], fsem.at[t]),
            pltpu.make_async_copy(mask_ref.at[t], mbuf.at[t], msem.at[t]),
        )

    for t in range(4):
        for cp in fetches(t):
            cp.start()
    fetch = pltpu.make_async_copy(mig_hbm, mig_ref, gsem)
    fetch.start()
    lane = lanes_of((N, N))

    def body(t, carry):
        for cp in fetches(t):
            cp.wait()
        wet = mbuf[t].astype(F32)
        for f in range(4):
            fbuf[t, f] = fbuf[t, f] * wet
        for f in range(NF):
            depth = 4 if f < 5 else 3
            low = 4 - depth
            tbuf[NORTH + 4 * f : NORTH + 4 * f + depth, :] = fbuf[t, f, 124 + low : 128, :]
            tbuf[SOUTH + 4 * f : SOUTH + 4 * f + depth, :] = fbuf[t, f, 0:depth, :]
            tbuf[NORTH_CORNER + 3 * f : NORTH_CORNER + 3 * f + depth - 1, :] = fbuf[t, f, 129 - depth : 128, :]
            tbuf[SOUTH_CORNER + 3 * f : SOUTH_CORNER + 3 * f + depth - 1, :] = fbuf[t, f, 0 : depth - 1, :]
        acc = jnp.transpose(tbuf[...])
        for f in range(NF):
            v = fbuf[t, f]
            acc = jnp.where((lane >= 8 * f) & (lane < 8 * f + 4), lane_roll(v, 8 * f), acc)
            acc = jnp.where((lane >= 8 * f + 4) & (lane < 8 * f + 8), lane_roll(v, 8 * f + 8), acc)
        out_ref[pl.ds(t, N, stride=4), :] = acc

        @pl.when(t == 0)
        def _():
            fetch.wait()

        @pl.when(mig_ref[0, lax.axis_index("curve")] == t)
        def _():
            pltpu.make_async_copy(fbuf.at[t], leave_ref, lsem).start()

        return carry

    lax.fori_loop(0, 4, body, 0)
    pltpu.make_async_copy(fbuf.at[0], leave_ref, lsem).wait()


def make_messages(mig, fields, mask):
    return pl.pallas_call(
        message_kernel,
        out_shape=(
            jax.ShapeDtypeStruct((4 * N, N), F32),
            jax.ShapeDtypeStruct((NF, N, N), F32),
        ),
        in_specs=[pl.BlockSpec(memory_space=pl.ANY)] * 3,
        out_specs=(pl.BlockSpec(memory_space=pltpu.VMEM), pl.BlockSpec(memory_space=pl.ANY)),
        scratch_shapes=[
            pltpu.VMEM((4, NF, N, N), F32),
            pltpu.VMEM((4, N, N), jnp.int32),
            pltpu.VMEM((N, N), F32),
            pltpu.SMEM((1, N), jnp.int32),
            pltpu.SemaphoreType.DMA((4,)),
            pltpu.SemaphoreType.DMA((4,)),
            pltpu.SemaphoreType.DMA,
            pltpu.SemaphoreType.DMA,
        ],
        compiler_params=pltpu.CompilerParams(vmem_limit_bytes=VMEM_ALL),
        cost_estimate=pl.CostEstimate(flops=2_000_000, bytes_accessed=3_000_000, transcendentals=0),
        name="messages",
    )(mig, fields, mask)


def route_kernel(near_hbm, mig_hbm, rows_hbm, out_ref, near_ref, mig_ref, table, picked, sem, osem):
    fetches = (
        pltpu.make_async_copy(near_hbm, near_ref, sem.at[0]),
        pltpu.make_async_copy(mig_hbm, mig_ref, sem.at[1]),
        pltpu.make_async_copy(rows_hbm, table, sem.at[2]),
    )
    for cp in fetches:
        cp.start()
    dev = lax.axis_index("curve")
    side = jnp.where(dev < N // 2, 4 * N, 0)
    lane = lanes_of((1, N))
    from_west = (lane < NORTH) & ((lane & 4) != 0)
    from_east = (lane < NORTH) & ((lane & 4) == 0)
    from_south = lane < SOUTH
    from_north = lane < NORTH_CORNER
    from_low = lane < SOUTH_CORNER
    for cp in fetches:
        cp.wait()

    def pick(p, place):
        s = near_ref[8 * N + p]
        n = near_ref[12 * N + p]
        row = table[pl.ds(near_ref[side + n], 1), :]
        row = jnp.where(from_low, table[pl.ds(near_ref[side + s], 1), :], row)
        row = jnp.where(from_north, table[pl.ds(n, 1), :], row)
        row = jnp.where(from_south, table[pl.ds(s, 1), :], row)
        row = jnp.where(from_east, table[pl.ds(near_ref[4 * N + p], 1), :], row)
        row = jnp.where(from_west, table[pl.ds(near_ref[p], 1), :], row)
        picked[pl.ds(place, 1), :] = row

    def body(d, carry):
        moving = mig_ref[d]
        first = 4 * d
        for i in range(3):
            pick(jnp.where(moving <= i, first + (i + 1), first + i), first + i)
        pick(first + moving, (first + 7) & (4 * N - 1))
        return carry

    lax.fori_loop(0, N, body, 0, unroll=4)
    give = pltpu.make_async_copy(picked, out_ref, osem)
    give.start()
    give.wait()


def route(near, mig, rows):
    hbm = pl.BlockSpec(memory_space=pl.ANY)
    return pl.pallas_call(
        route_kernel,
        out_shape=jax.ShapeDtypeStruct((4 * N, N), F32),
        in_specs=[hbm] * 3,
        out_specs=hbm,
        scratch_shapes=[
            pltpu.SMEM((16 * N,), jnp.int32),
            pltpu.SMEM((N,), jnp.int32),
            pltpu.VMEM((4 * N, N), F32),
            pltpu.VMEM((4 * N, N), F32),
            pltpu.SemaphoreType.DMA((3,)),
            pltpu.SemaphoreType.DMA,
        ],
        compiler_params=pltpu.CompilerParams(vmem_limit_bytes=VMEM_ALL),
        cost_estimate=pl.CostEstimate(flops=2_000_000, bytes_accessed=2_000_000, transcendentals=0),
        name="route",
    )(near, mig, rows)


def own_strips(patch, i, lane, cols, rows):
    east = (lane >= 32 * i + 4) & (lane < 32 * i + 12)
    west = (lane >= 32 * i + 20) & (lane < 32 * i + 28)
    for f in range(NF):
        v = patch[f]
        old = jnp.where(east, pltpu.roll(v, (32 * i + 12) & (N - 1), 1), cols[f])
        cols[f] = jnp.where(west, pltpu.roll(v, (32 * i + 20) & (N - 1), 1), old)
        rows[pl.ds((f * KR + 4) * SUB + 2 * i, 8, stride=SUB), :] = patch[f, 0:8, :]
        rows[pl.ds((f * KR) * SUB + 2 * i + 1, 8, stride=SUB), :] = patch[f, 120:128, :]


def interior(patch, work, terms):
    for f in range(NF):
        for j in range(JM):
            work[0, f, j] = patch[f, pl.ds(j, SUB, stride=JM), :]
            if f == 5:
                work[1, f, j] = work[0, f, j]

    def step(k, carry):
        a, b = k & 1, 1 - (k & 1)

        def load(j, f):
            return work[a, f, j]

        def store(j, f, value):
            work[b, f, j] = value

        advance_tiles(load, store, terms, 0, JM, JM)
        return carry

    lax.fori_loop(0, 4, step, 0)
    for f in range(5):
        for j in range(JM):
            patch[f, pl.ds(j, SUB, stride=JM), :] = work[0, f, j]


def interior_kernel(arrival, refs):
    mig_hbm, fields_ref, mask_ref = refs[:3]
    if arrival:
        come_ref, cols_in, rows_in = refs[3:6]
        out_ref, cols_ref, rows_ref = refs[6:9]
    else:
        near_ref = refs[3]
        out_ref, cols_ref, rows_ref, known_ref = refs[4:8]
    fbuf, mbuf, work, terms, cols, rows, mig_ref, near_buf, known, fsem, msem, csem, osem, gsem = refs[-14:]
    first = 2 if arrival else 0
    slots = 2 if arrival else 3
    come = slots

    def fetches(n):
        return (
            pltpu.make_async_copy(fields_ref.at[first + n], fbuf.at[n], fsem.at[n]),
            pltpu.make_async_copy(mask_ref.at[first + n], mbuf.at[n], msem.at[n]),
        )

    fetch_mig = pltpu.make_async_copy(mig_hbm, mig_ref, gsem.at[0])
    fetch_mig.start()
    for n in range(slots):
        for cp in fetches(n):
            cp.start()
    if arrival:
        given = (
            pltpu.make_async_copy(cols_in, cols, csem.at[0]),
            pltpu.make_async_copy(rows_in, rows, csem.at[1]),
            pltpu.make_async_copy(come_ref, fbuf.at[come], fsem.at[come]),
        )
        for cp in given:
            cp.start()
    else:
        fetch_near = pltpu.make_async_copy(near_ref, near_buf, gsem.at[1])
        fetch_near.start()
        cols[...] = jnp.zeros(cols.shape, F32)
        rows[...] = jnp.zeros(rows.shape, F32)
    fetch_mig.wait()
    moving = mig_ref[0, lax.axis_index("curve")]
    if not arrival:
        fetch_near.wait()
        for k in range(4):
            for c in range(4):
                known[4 * k + c : 4 * k + c + 1, :] = jnp.maximum(near_buf[k : k + 1, c * N : (c + 1) * N], 0)
        give = pltpu.make_async_copy(known, known_ref, gsem.at[1])
        give.start()
    lane = lanes_of((N, N))

    def mask_patch(n):
        wet = mbuf[n].astype(F32)
        for f in range(4):
            fbuf[n, f] = fbuf[n, f] * wet

    def place_of(n):
        place = n + (moving <= first + n).astype(jnp.int32)
        return jnp.where(n == 1, come, place) if arrival else place

    def run(n, carry):
        place = place_of(n)

        @pl.when(n == 0)
        def _():
            for t in range(slots):
                for cp in fetches(t):
                    cp.wait()
            if arrival:
                for cp in given:
                    cp.wait()

        if arrival:

            @pl.when(n == 0)
            def _():
                mask_patch(place)
        else:
            mask_patch(place)
        patch = fbuf.at[place]
        own_strips(patch, first + n, lane, cols, rows)
        interior(patch, work, terms)
        pltpu.make_async_copy(patch, out_ref.at[n], osem.at[n]).start()
        return carry

    lax.fori_loop(0, 2, run, 0)
    last = (
        pltpu.make_async_copy(cols, cols_ref, csem.at[0]),
        pltpu.make_async_copy(rows, rows_ref, csem.at[1]),
    )
    for cp in last:
        cp.start()
    for n in range(2):
        pltpu.make_async_copy(fbuf.at[n], out_ref.at[n], osem.at[n]).wait()
    for cp in last:
        cp.wait()
    if not arrival:
        give.wait()


def interiors(arrival, name, mig, fields, mask, *more):
    hbm = pl.BlockSpec(memory_space=pl.ANY)

    def kernel(*refs):
        interior_kernel(arrival, refs)

    return pl.pallas_call(
        kernel,
        out_shape=(
            jax.ShapeDtypeStruct((2, NF, N, N), F32),
            jax.ShapeDtypeStruct((NF, N, N), F32),
            jax.ShapeDtypeStruct((NF * KR * SUB, N), F32),
        )
        + (() if arrival else (jax.ShapeDtypeStruct((16, N), jnp.int32),)),
        in_specs=[hbm] * (3 + len(more)),
        out_specs=(hbm,) * (3 if arrival else 4),
        scratch_shapes=[
            pltpu.VMEM((3, NF, N, N), F32),
            pltpu.VMEM((3, N, N), jnp.int32),
            pltpu.VMEM((2, NF, JM, SUB, N), F32),
            pltpu.VMEM((TERMS, JM, SUB, N), F32),
            pltpu.VMEM((NF, N, N), F32),
            pltpu.VMEM((NF * KR * SUB, N), F32),
            pltpu.SMEM((1, N), jnp.int32),
            pltpu.VMEM((4, 4 * N), jnp.int32),
            pltpu.VMEM((16, N), jnp.int32),
            pltpu.SemaphoreType.DMA((3,)),
            pltpu.SemaphoreType.DMA((3,)),
            pltpu.SemaphoreType.DMA((2,)),
            pltpu.SemaphoreType.DMA((2,)),
            pltpu.SemaphoreType.DMA((2,)),
        ],
        compiler_params=pltpu.CompilerParams(vmem_limit_bytes=VMEM_ALL),
        cost_estimate=pl.CostEstimate(flops=60_000_000, bytes_accessed=1_600_000, transcendentals=0),
        name=name,
    )(mig, fields, mask, *more)


def finish_kernel(
    near_hbm, mig_hbm, halo_hbm, cols_ref, rows_ref, low_ref, high_ref, out_ref,
    near_ref, mig_ref, halo_ref, wide, own, flip, cwork, rwork, terms, stage, isem, ssem, osem, nsem,
):
    fetch_halo = pltpu.make_async_copy(halo_hbm, halo_ref, nsem.at[0])
    fetch_near = pltpu.make_async_copy(near_hbm, near_ref, nsem.at[1])
    fetch_mig = pltpu.make_async_copy(mig_hbm, mig_ref, nsem.at[2])
    fetch_halo.start()
    fetch_near.start()
    fetch_mig.start()
    fetch_cols = pltpu.make_async_copy(cols_ref, own, isem.at[0])
    fetch_rows = pltpu.make_async_copy(rows_ref, rwork.at[0], isem.at[1])
    fetch_cols.start()
    fetch_rows.start()
    fetch_low = pltpu.make_async_copy(low_ref, stage.at[0:2], ssem.at[0])
    fetch_high = pltpu.make_async_copy(high_ref, stage.at[2:4], ssem.at[1])
    fetch_low.start()
    fetch_high.start()
    lane_all = lanes_of((N, N))
    fetch_halo.wait()

    def halo_columns(f, carry):
        acc = jnp.zeros((N, N), F32)
        for i in range(4):
            moved = pltpu.roll(halo_ref[pl.ds(i, N, stride=4), :], (32 * i + 12 - 8 * f) & (N - 1), 1)
            acc = moved if i == 0 else jnp.where(lane_all >= 32 * i, moved, acc)
        wide[f, 4 : 4 + N, :] = acc
        return carry

    lax.fori_loop(0, NF, halo_columns, 0)
    fetch_cols.wait()
    fetch_rows.wait()

    def own_columns(f, carry):
        inside = ((lane_all & 31) >= 12) & ((lane_all & 31) < 20)
        wide[f, 4 : 4 + N, :] = jnp.where(inside, wide[f, 4 : 4 + N, :], own[f])
        return carry

    lax.fori_loop(0, NF, own_columns, 0)
    lane4 = lanes_of((4, N))
    low_half = lane4 < N // 2
    flip[N:136, :] = jnp.zeros((8, N), F32)

    def halo_rows(i, carry):
        flip[0:N, :] = jnp.transpose(halo_ref[pl.ds(i, N, stride=4), :])
        here = lane4 // 32 == i
        for f in range(NF):
            for high in range(2):
                if high:
                    edge = flip[SOUTH + 4 * f : SOUTH + 4 * f + 4, :]
                    corner = flip[SOUTH_CORNER + 3 * f : SOUTH_CORNER + 3 * f + 4, :]
                else:
                    shift = 0 if f < 5 else 1
                    edge = flip[NORTH + 4 * f - shift : NORTH + 4 * f - shift + 4, :]
                    start = NORTH_CORNER - 1 + 3 * f if f < 5 else NORTH_CORNER + 13
                    corner = flip[start : start + 4, :]
                a = pltpu.roll(jnp.where(low_half, corner, edge), (32 * i + 12) & (N - 1), 1)
                b = pltpu.roll(jnp.where(low_half, edge, corner), (32 * i + 20) & (N - 1), 1)
                ends = jnp.where((lane4 & 31) < 16, a, b)
                at = 132 if high else 0
                wide[f, at : at + 4, :] = jnp.where(here, ends, wide[f, at : at + 4, :])
                k0 = 8 if high else 0
                for r in range(4):
                    rwork[0, f, k0 + r, pl.ds(2 * i + high, 1), :] = edge[r : r + 1, :]
        return carry

    lax.fori_loop(0, 4, halo_rows, 0)

    def arrange(f, carry):
        for j in range(JC):
            cwork[0, f, j] = wide[f, pl.ds(j, SUB, stride=JC), :]
        return carry

    lax.fori_loop(0, NF, arrange, 0)

    fetch_near.wait()
    fetch_mig.wait()
    dev = lax.axis_index("curve")
    moving = mig_ref[0, dev]
    before = (dev + N - 1) & (N - 1)
    lane = lanes_of((SUB, N))
    sub = subs_of((SUB, N))
    group = lane // 32

    lacks = []
    for i in range(4):
        patch = 4 * dev + slot_of(i, moving) if i < 3 else 4 * before + mig_ref[0, before]
        lacks.append([(near_ref[k, patch] < 0).astype(jnp.int32) for k in range(4)])

    def by_group(k):
        v = jnp.zeros((SUB, N), jnp.int32)
        for i in range(4):
            v = jnp.where(group == i, lacks[i][k], v)
        return v != 0

    in_group = lane & 31
    no_west, no_east, no_south, no_north = (by_group(k) for k in range(4))
    source = jnp.where(no_west & ((in_group == 18) | (in_group == 19)), lane - in_group + 20, lane)
    source = jnp.where(no_east & ((in_group == 12) | (in_group == 13)), lane - in_group + 11, source)
    low_fix = no_south & (sub == 0)
    high_fix = no_north & (sub == 7)
    row_flag = jnp.zeros((SUB, N), jnp.int32)
    for i in range(4):
        row_flag = jnp.where(sub == 2 * i, lacks[i][2], row_flag)
        row_flag = jnp.where(sub == 2 * i + 1, lacks[i][3], row_flag)
    row_low = (row_flag != 0) & ((sub & 1) == 0)
    row_high = (row_flag != 0) & ((sub & 1) == 1)

    def edge(f, carry):
        for j in range(JC):
            cwork[0, f, j] = jnp.take_along_axis(cwork[0, f, j], source, axis=1, mode="promise_in_bounds")
        for j in (2, 3):
            cwork[0, f, j] = jnp.where(low_fix, cwork[0, f, 4], cwork[0, f, j])
        for j in (13, 14):
            cwork[0, f, j] = jnp.where(high_fix, cwork[0, f, 12], cwork[0, f, j])
        return carry

    def step(k, carry):
        @pl.when(k == 0)
        def _():
            lax.fori_loop(0, NF, edge, 0)
            for j in range(JC):
                cwork[1, 5, j] = cwork[0, 5, j]

        @pl.when(k == 2)
        def _():
            lax.fori_loop(0, 5, edge, 0)

        a, b = k & 1, 1 - (k & 1)

        def load(j, f):
            return cwork[a, f, j]

        def store(j, f, value):
            cwork[b, f, j] = value

        advance_tiles(load, store, terms, 0, JC, JC)
        return carry

    lax.fori_loop(0, 4, step, 0)

    def row_edges(fields):
        for f in fields:
            for k in (2, 3):
                rwork[0, f, k] = jnp.where(row_low, rwork[0, f, 4], rwork[0, f, k])
            for k in (8, 9):
                rwork[0, f, k] = jnp.where(row_high, rwork[0, f, 7], rwork[0, f, k])

    row_edges((5,))
    for j in range(KR):
        rwork[1, 5, j] = rwork[0, 5, j]

    def row_step(k, carry):
        @pl.when((k & 1) == 0)
        def _():
            row_edges(range(5))

        a, b = k & 1, 1 - (k & 1)

        def load(j, f):
            return rwork[a, f, j]

        def store(j, f, value):
            rwork[b, f, j] = value

        @pl.when(k < 2)
        def _():
            advance_tiles(load, store, terms, 1, 11, KR)

        @pl.when(k >= 2)
        def _():
            advance_tiles(load, store, terms, 3, 9, KR)

        return carry

    lax.fori_loop(0, 4, row_step, 0)

    def restore(f, carry):
        for j in range(JC):
            wide[f, pl.ds(j, SUB, stride=JC), :] = cwork[0, f, j]
        return carry

    lax.fori_loop(0, 5, restore, 0)
    fetch_low.wait()
    fetch_high.wait()

    def put_out(i):
        slot = jnp.where(i == 3, moving, i + (moving <= i).astype(jnp.int32))
        return pltpu.make_async_copy(stage.at[i], out_ref.at[slot], osem.at[i])

    def merge(i, carry):
        for f in range(5):
            for r in range(4):
                stage[i, f, r : r + 1, :] = rwork[0, f, 4 + r, pl.ds(2 * i, 1), :]
                stage[i, f, 124 + r : 125 + r, :] = rwork[0, f, 4 + r, pl.ds(2 * i + 1, 1), :]
            strip = wide[f, 4 : 4 + N, :]
            v = jnp.where(lane_all < 4, pltpu.roll(strip, (236 - 32 * i) & (N - 1), 1), stage[i, f])
            stage[i, f] = jnp.where(lane_all >= 124, pltpu.roll(strip, 116 - 32 * i, 1), v)
        put_out(i).start()
        return carry

    lax.fori_loop(0, 4, merge, 0)
    for i in range(4):
        put_out(i).wait()


def finish(near, mig, halo, cols, rows, low, high):
    hbm = pl.BlockSpec(memory_space=pl.ANY)
    return pl.pallas_call(
        finish_kernel,
        out_shape=jax.ShapeDtypeStruct((4, NF, N, N), F32),
        in_specs=[hbm] * 7,
        out_specs=hbm,
        scratch_shapes=[
            pltpu.SMEM((4, 4 * N), jnp.int32),
            pltpu.SMEM((1, N), jnp.int32),
            pltpu.VMEM((4 * N, N), F32),
            pltpu.VMEM((NF, 136, N), F32),
            pltpu.VMEM((NF, N, N), F32),
            pltpu.VMEM((136, N), F32),
            pltpu.VMEM((2, NF, JC, SUB, N), F32),
            pltpu.VMEM((2, NF, KR, SUB, N), F32),
            pltpu.VMEM((TERMS, JC, SUB, N), F32),
            pltpu.VMEM((4, NF, N, N), F32),
            pltpu.SemaphoreType.DMA((2,)),
            pltpu.SemaphoreType.DMA((2,)),
            pltpu.SemaphoreType.DMA((4,)),
            pltpu.SemaphoreType.DMA((3,)),
        ],
        compiler_params=pltpu.CompilerParams(vmem_limit_bytes=VMEM_ALL),
        cost_estimate=pl.CostEstimate(flops=30_000_000, bytes_accessed=3_000_000, transcendentals=0),
        name="finish",
    )(near, mig, halo, cols, rows, low, high)


def swap(rows):
    return lax.all_to_all(rows.reshape(N, 4, N), "curve", 0, 0, tiled=True).reshape(4 * N, N)


def shards(fields, wet_mask, neighbors, migration):
    near, mig = neighbors.T, migration.T
    owners = lax.axis_size("curve")
    messages, leaving = make_messages(mig, fields, wet_mask)
    spread = swap(messages)
    patch = lax.ppermute(leaving, "curve", [(d, (d + 1) % owners) for d in range(owners)])
    low, cols, rows, known = interiors(False, "first", mig, fields, wet_mask, near)
    halo = swap(route(known.reshape(16 * N), migration.reshape(N), spread))
    high, cols, rows = interiors(True, "second", mig, fields, wet_mask, patch, cols, rows)
    return finish(near, mig, halo, cols, rows.reshape(NF, KR, SUB, N), low, high)


def solution(mesh):
    placed = (P("curve", None, None, None), P("curve", None, None), P(), P())
    return jax.shard_map(
        shards, mesh=mesh, in_specs=placed, out_specs=P("curve", None, None, None), check_vma=False
    )
```

```python
import jax
import jax.numpy as jnp
from jax import lax
from jax.experimental import pallas as pl
from jax.experimental.pallas import tpu as pltpu
from jax.sharding import PartitionSpec as P

GRAVITY = 9.81
TIME_STEP = 0.04
DRY_EPS = 0.01
CAPACITY = 0.02
EROSION = 0.5
SETTLING = 0.2
POROSITY = 0.4

F32 = jnp.float32
NF = 6
N = 128
SUB = 8
JM = 16
JC = 17
KR = 12
VMEM_ALL = 67_043_328

NORTH, SOUTH, NORTH_CORNER, SOUTH_CORNER = 48, 71, 94, 111


def lanes_of(shape):
    return lax.broadcasted_iota(jnp.int32, shape, 1)


def subs_of(shape):
    return lax.broadcasted_iota(jnp.int32, shape, 0)


def lane_pick(v, index):
    return jnp.take_along_axis(v, index, axis=1, mode="promise_in_bounds")


def to_the_east(v):
    return pltpu.roll(v, N - 1, 1)


def to_the_west(v):
    return pltpu.roll(v, 1, 1)


def root(x):
    return x * lax.rsqrt(x)


def root_from_zero(x):
    return root(jnp.maximum(x, 1e-30))


def cell_terms(h, qx, qy, m):
    hp = jnp.maximum(h, 0.0)
    h2 = h * h
    a = h / (h2 + DRY_EPS)
    u, v, s = qx * a, qy * a, m * a
    r = root(hp + 0.01)
    half = (0.5 * GRAVITY) * h2
    return dict(
        h=h, hp=hp, qx=qx, qy=qy, m=m, r=r, ru=r * u, rv=r * v, rs=r * s,
        fxx=qx * u + half, fxy=qx * v, fyy=qy * v + half, fxs=qx * s, fys=qy * s,
    )


ROLLED_X = ("h", "qx", "qy", "m", "r", "ru", "rv", "rs", "fxx", "fxy", "fxs")


def face_twice(L, R, along_x):
    qn, qt, rn, rt, fn, fs = (
        ("qx", "qy", "ru", "rv", "fxx", "fxs") if along_x else ("qy", "qx", "rv", "ru", "fyy", "fys")
    )
    c = root_from_zero((0.5 * GRAVITY) * (L["hp"] + R["hp"])) + 0.1
    iw, ic2 = 1.0 / (L["r"] + R["r"]), 1.0 / (c + c)
    U = (L[rn] + R[rn]) * iw
    W = (L[rt] + R[rt]) * iw
    S = (L["rs"] + R["rs"]) * iw
    dh = R["h"] - L["h"]
    dn = R[qn] - L[qn]
    dt = R[qt] - L[qt]
    dm = R["m"] - L["m"]
    up, um = U + c, U - c
    p1 = jnp.abs(um) * ((up * dh - dn) * ic2)
    p3 = jnp.abs(up) * ((dn - um * dh) * ic2)
    mid = jnp.abs(U)
    b = p1 + p3
    f_h = (L[qn] + R[qn]) - b
    f_n = (L[fn] + R[fn]) - (p1 * um + p3 * up)
    e = b - mid * dh
    f_t = (L["fxy"] + R["fxy"]) - (W * e + mid * dt)
    f_s = (L[fs] + R[fs]) - (S * e + mid * dm)
    return f_h, f_n, f_t, f_s


def update(C, bed, bed_e, bed_w, bed_n, bed_s, fric, dx, fyn, fys):
    k = 0.5 * TIME_STEP
    h = C["h"]
    slope = (TIME_STEP * GRAVITY * 0.5) * h
    nh = h - k * (dx[0] + (fyn[0] - fys[0]))
    nx = C["qx"] - k * (dx[1] + (fyn[2] - fys[2])) - slope * (bed_e - bed_w)
    ny = C["qy"] - k * (dx[2] + (fyn[1] - fys[1])) - slope * (bed_n - bed_s)
    nm = C["m"] - k * (dx[3] + (fyn[3] - fys[3]))
    a = nh / (nh * nh + DRY_EPS)
    vx, vy = nx * a, ny * a
    speed2 = vx * vx + vy * vy
    speed = root_from_zero(speed2)
    depth = jnp.maximum(nh, 0.0) + 0.1
    factor = depth / (depth + (TIME_STEP * fric) * speed)
    conc = nm * a
    net = EROSION * jnp.maximum(CAPACITY * speed2 - conc, 0.0) - SETTLING * conc
    nm = nm + TIME_STEP * net
    nb = bed - (TIME_STEP / (1.0 - POROSITY)) * net
    return nh, nx * factor, ny * factor, nm, nb


KEPT = ("r", "ru", "rv", "rs", "fxy", "fyy", "fys", "fxx", "fxs")
FLUX = len(KEPT)
MOVED = FLUX + 4
TERMS = MOVED + len(ROLLED_X)


def x_terms(load, terms, j, faces):
    cur = cell_terms(*(load(j, f) for f in range(4)))
    for n, key in enumerate(KEPT):
        terms[n, j] = cur[key]
    if faces:
        for n, key in enumerate(ROLLED_X):
            terms[MOVED + n, j] = to_the_east(cur[key])


def x_faces(load, terms, j):
    L = {key: load(j, f) for f, key in enumerate(("h", "qx", "qy", "m"))}
    for n, key in enumerate(KEPT):
        L[key] = terms[n, j]
    R = {key: terms[MOVED + n, j] for n, key in enumerate(ROLLED_X)}
    for C in (L, R):
        C["hp"] = jnp.maximum(C["h"], 0.0)
    east = face_twice(L, R, True)
    for n in range(4):
        terms[FLUX + n, j] = east[n]


def y_pass(load, store, terms, lo, hi, last):
    wraps = lo == 0

    def around(j, get):
        if j < 0:
            return pltpu.roll(get(last - 1), 1, 0)
        if j == last:
            return pltpu.roll(get(0), SUB - 1, 0)
        return get(j)

    def cell(j):
        C = {key: around(j, lambda t: load(t, f)) for f, key in enumerate(("h", "qx", "qy", "m"))}
        for n, key in enumerate(KEPT):
            C[key] = around(j, lambda t: terms[n, t])
        C["hp"] = jnp.maximum(C["h"], 0.0)
        return C

    if wraps:
        top = face_twice(cell(last - 1), cell(last), False)
        south = tuple(pltpu.roll(x, 1, 0) for x in top)
    else:
        south = face_twice(cell(lo - 1), cell(lo), False)
    cur = cell(lo)
    for j in range(lo, hi):
        if wraps and j == last - 1:
            nxt, north = None, top
        else:
            nxt = cell(j + 1)
            north = face_twice(cur, nxt, False)
        bed = load(j, 4)
        dx = tuple(terms[FLUX + n, j] - to_the_west(terms[FLUX + n, j]) for n in range(4))
        bed_n, bed_s = (around(t, lambda t: load(t, 4)) for t in (j + 1, j - 1))
        new = update(
            cur, bed, to_the_east(bed), to_the_west(bed), bed_n, bed_s, load(j, 5), dx, north, south,
        )
        for f in range(5):
            store(j, f, new[f])
        south = north
        cur = cell(j + 1) if j + 1 < hi else None


def advance_tiles(load, store, terms, lo, hi, last):
    span = range(last) if lo == 0 else range(lo - 1, hi + 1)
    for j in span:
        x_terms(load, terms, j, lo <= j < hi)
    for j in range(lo, hi):
        x_faces(load, terms, j)
    y_pass(load, store, terms, lo, hi, last)


def slot_of(i, moving):
    if i == 3:
        return moving
    return i + (moving <= i).astype(jnp.int32)


def message_kernel(mig_hbm, fields_ref, mask_ref, out_ref, leave_ref, fbuf, mbuf, tbuf, mig_ref, fsem, msem, gsem, lsem):
    def fetches(t):
        return (
            pltpu.make_async_copy(fields_ref.at[t], fbuf.at[t], fsem.at[t]),
            pltpu.make_async_copy(mask_ref.at[t], mbuf.at[t], msem.at[t]),
        )

    for t in range(4):
        for cp in fetches(t):
            cp.start()
    fetch = pltpu.make_async_copy(mig_hbm, mig_ref, gsem)
    fetch.start()
    lane = lanes_of((N, N))
    edge_lane = (lane & 3) + jnp.where((lane & 4) != 0, 124, 0)

    def body(t, carry):
        for cp in fetches(t):
            cp.wait()
        wet = mbuf[t].astype(F32)
        for f in range(4):
            fbuf[t, f] = fbuf[t, f] * wet
        for f in range(NF):
            depth = 4 if f < 5 else 3
            low = 4 - depth
            tbuf[NORTH + 4 * f : NORTH + 4 * f + depth, :] = fbuf[t, f, 124 + low : 128, :]
            tbuf[SOUTH + 4 * f : SOUTH + 4 * f + depth, :] = fbuf[t, f, 0:depth, :]
            tbuf[NORTH_CORNER + 3 * f : NORTH_CORNER + 3 * f + depth - 1, :] = fbuf[t, f, 129 - depth : 128, :]
            tbuf[SOUTH_CORNER + 3 * f : SOUTH_CORNER + 3 * f + depth - 1, :] = fbuf[t, f, 0 : depth - 1, :]
        acc = jnp.transpose(tbuf[...])
        for f in range(NF):
            v = fbuf[t, f]
            acc = jnp.where((lane >= 8 * f) & (lane < 8 * f + 8), lane_pick(v, edge_lane), acc)
        out_ref[pl.ds(t, N, stride=4), :] = acc

        @pl.when(t == 0)
        def _():
            fetch.wait()

        @pl.when(mig_ref[0, lax.axis_index("curve")] == t)
        def _():
            pltpu.make_async_copy(fbuf.at[t], leave_ref, lsem).start()

        return carry

    lax.fori_loop(0, 4, body, 0)
    pltpu.make_async_copy(fbuf.at[0], leave_ref, lsem).wait()


def make_messages(mig, fields, mask):
    return pl.pallas_call(
        message_kernel,
        out_shape=(
            jax.ShapeDtypeStruct((4 * N, N), F32),
            jax.ShapeDtypeStruct((NF, N, N), F32),
        ),
        in_specs=[pl.BlockSpec(memory_space=pl.ANY)] * 3,
        out_specs=(pl.BlockSpec(memory_space=pltpu.VMEM), pl.BlockSpec(memory_space=pl.ANY)),
        scratch_shapes=[
            pltpu.VMEM((4, NF, N, N), F32),
            pltpu.VMEM((4, N, N), jnp.int32),
            pltpu.VMEM((N, N), F32),
            pltpu.SMEM((1, N), jnp.int32),
            pltpu.SemaphoreType.DMA((4,)),
            pltpu.SemaphoreType.DMA((4,)),
            pltpu.SemaphoreType.DMA,
            pltpu.SemaphoreType.DMA,
        ],
        compiler_params=pltpu.CompilerParams(vmem_limit_bytes=VMEM_ALL),
        cost_estimate=pl.CostEstimate(flops=2_000_000, bytes_accessed=3_000_000, transcendentals=0),
        name="messages",
    )(mig, fields, mask)


def route_kernel(w_hbm, e_hbm, s_hbm, n_hbm, side_hbm, mig_hbm, rows_hbm, out_ref, w_ref, e_ref, s_ref, n_ref, side_ref, mig_ref, table, picked, sem, osem):
    fetches = tuple(
        pltpu.make_async_copy(a, b, sem.at[k])
        for k, (a, b) in enumerate(
            (
                (w_hbm, w_ref), (e_hbm, e_ref), (s_hbm, s_ref), (n_hbm, n_ref),
                (side_hbm, side_ref), (mig_hbm, mig_ref), (rows_hbm, table),
            )
        )
    )
    for cp in fetches:
        cp.start()
    lane = lanes_of((1, N))
    from_west = (lane < NORTH) & ((lane & 4) != 0)
    from_east = (lane < NORTH) & ((lane & 4) == 0)
    from_south = lane < SOUTH
    from_north = lane < NORTH_CORNER
    from_low = lane < SOUTH_CORNER
    for cp in fetches:
        cp.wait()

    def pick(p, place):
        s, n = s_ref[p], n_ref[p]
        row = table[pl.ds(side_ref[n], 1), :]
        row = jnp.where(from_low, table[pl.ds(side_ref[s], 1), :], row)
        row = jnp.where(from_north, table[pl.ds(n, 1), :], row)
        row = jnp.where(from_south, table[pl.ds(s, 1), :], row)
        row = jnp.where(from_east, table[pl.ds(e_ref[p], 1), :], row)
        row = jnp.where(from_west, table[pl.ds(w_ref[p], 1), :], row)
        picked[pl.ds(place, 1), :] = row

    def body(d, carry):
        moving = mig_ref[d]
        first = 4 * d
        for i in range(3):
            pick(jnp.where(moving <= i, first + (i + 1), first + i), first + i)
        pick(first + moving, (first + 7) & (4 * N - 1))
        return carry

    lax.fori_loop(0, N, body, 0, unroll=4)
    give = pltpu.make_async_copy(picked, out_ref, osem)
    give.start()
    give.wait()


def route(tables, mig, rows):
    hbm = pl.BlockSpec(memory_space=pl.ANY)
    return pl.pallas_call(
        route_kernel,
        out_shape=jax.ShapeDtypeStruct((4 * N, N), F32),
        in_specs=[hbm] * 7,
        out_specs=hbm,
        scratch_shapes=[
            *(pltpu.SMEM((4 * N,), jnp.int32) for _ in range(5)),
            pltpu.SMEM((N,), jnp.int32),
            pltpu.VMEM((4 * N, N), F32),
            pltpu.VMEM((4 * N, N), F32),
            pltpu.SemaphoreType.DMA((7,)),
            pltpu.SemaphoreType.DMA,
        ],
        compiler_params=pltpu.CompilerParams(vmem_limit_bytes=VMEM_ALL),
        cost_estimate=pl.CostEstimate(flops=2_000_000, bytes_accessed=2_000_000, transcendentals=0),
        name="route",
    )(*tables, mig, rows)


def own_strips(patch, i, lane, cols, rows):
    at = lane - 32 * i
    inside = (at >= 4) & (at < 28)
    source = jnp.where(at < 16, at + 116, at - 20) & (N - 1)
    for f in range(NF):
        v = patch[f]
        cols[f] = jnp.where(inside, lane_pick(v, source), cols[f])
        rows[pl.ds((f * KR + 4) * SUB + 2 * i, 8, stride=SUB), :] = patch[f, 0:8, :]
        rows[pl.ds((f * KR) * SUB + 2 * i + 1, 8, stride=SUB), :] = patch[f, 120:128, :]


def interior(patch, work, terms):
    for f in range(NF):
        for j in range(JM):
            work[0, f, j] = patch[f, pl.ds(j, SUB, stride=JM), :]
            if f == 5:
                work[1, f, j] = work[0, f, j]

    def step(k, carry):
        a, b = k & 1, 1 - (k & 1)

        def load(j, f):
            return work[a, f, j]

        def store(j, f, value):
            work[b, f, j] = value

        advance_tiles(load, store, terms, 0, JM, JM)
        return carry

    lax.fori_loop(0, 4, step, 0)
    for f in range(5):
        for j in range(JM):
            patch[f, pl.ds(j, SUB, stride=JM), :] = work[0, f, j]


def interior_kernel(arrival, refs):
    mig_hbm, fields_ref, mask_ref = refs[:3]
    if arrival:
        come_ref, cols_in, rows_in = refs[3:6]
        out_ref, cols_ref, rows_ref = refs[6:9]
    else:
        near_ref, leave_ref = refs[3:5]
        out_ref, cols_ref, rows_ref, passed_ref = refs[5:9]
        known_refs = refs[9:14]
        del leave_ref, passed_ref
    fbuf, mbuf, work, terms, cols, rows, mig_ref, near_buf, known, fsem, msem, csem, osem, gsem, ksem = refs[-15:]
    first = 2 if arrival else 0
    slots = 2 if arrival else 3
    come = slots

    def fetches(n):
        return (
            pltpu.make_async_copy(fields_ref.at[first + n], fbuf.at[n], fsem.at[n]),
            pltpu.make_async_copy(mask_ref.at[first + n], mbuf.at[n], msem.at[n]),
        )

    fetch_mig = pltpu.make_async_copy(mig_hbm, mig_ref, gsem.at[0])
    fetch_mig.start()
    for n in range(slots):
        for cp in fetches(n):
            cp.start()
    if arrival:
        given = (
            pltpu.make_async_copy(cols_in, cols, csem.at[0]),
            pltpu.make_async_copy(rows_in, rows, csem.at[1]),
            pltpu.make_async_copy(come_ref, fbuf.at[come], fsem.at[come]),
        )
        for cp in given:
            cp.start()
    else:
        fetch_near = pltpu.make_async_copy(near_ref, near_buf, gsem.at[1])
        fetch_near.start()
        cols[...] = jnp.zeros(cols.shape, F32)
        rows[...] = jnp.zeros(rows.shape, F32)
    fetch_mig.wait()
    moving = mig_ref[0, lax.axis_index("curve")]
    if not arrival:
        fetch_near.wait()
        for c in range(4):
            part = [jnp.maximum(near_buf[k : k + 1, c * N : (c + 1) * N], 0) for k in range(4)]
            part.append(jnp.where(lax.axis_index("curve") < N // 2, part[1], part[0]))
            for k in range(5):
                known[k, c : c + 1, :] = part[k]
        give = [pltpu.make_async_copy(known.at[k], known_refs[k], ksem.at[k]) for k in range(5)]
        for cp in give:
            cp.start()
    lane = lanes_of((N, N))

    def mask_patch(n):
        wet = mbuf[n].astype(F32)
        for f in range(4):
            fbuf[n, f] = fbuf[n, f] * wet

    def place_of(n):
        place = n + (moving <= first + n).astype(jnp.int32)
        return jnp.where(n == 1, come, place) if arrival else place

    def run(n, carry):
        place = place_of(n)

        @pl.when(n == 0)
        def _():
            for t in range(slots):
                for cp in fetches(t):
                    cp.wait()
            if arrival:
                for cp in given:
                    cp.wait()

        if arrival:

            @pl.when(n == 0)
            def _():
                mask_patch(place)
        else:
            mask_patch(place)
        patch = fbuf.at[place]
        own_strips(patch, first + n, lane, cols, rows)
        interior(patch, work, terms)
        pltpu.make_async_copy(patch, out_ref.at[n], osem.at[n]).start()
        return carry

    lax.fori_loop(0, 2, run, 0)
    last = (
        pltpu.make_async_copy(cols, cols_ref, csem.at[0]),
        pltpu.make_async_copy(rows, rows_ref, csem.at[1]),
    )
    for cp in last:
        cp.start()
    for n in range(2):
        pltpu.make_async_copy(fbuf.at[n], out_ref.at[n], osem.at[n]).wait()
    for cp in last:
        cp.wait()
    if not arrival:
        for cp in give:
            cp.wait()


def interiors(arrival, name, mig, fields, mask, *more):
    hbm = pl.BlockSpec(memory_space=pl.ANY)

    def kernel(*refs):
        interior_kernel(arrival, refs)

    return pl.pallas_call(
        kernel,
        out_shape=(
            jax.ShapeDtypeStruct((2, NF, N, N), F32),
            jax.ShapeDtypeStruct((NF, N, N), F32),
            jax.ShapeDtypeStruct((NF * KR * SUB, N), F32),
        )
        + (() if arrival else (jax.ShapeDtypeStruct((NF, N, N), F32),) + (jax.ShapeDtypeStruct((4, N), jnp.int32),) * 5),
        in_specs=[hbm] * (3 + len(more)),
        out_specs=(hbm,) * (3 if arrival else 9),
        input_output_aliases={} if arrival else {4: 3},
        scratch_shapes=[
            pltpu.VMEM((3, NF, N, N), F32),
            pltpu.VMEM((3, N, N), jnp.int32),
            pltpu.VMEM((2, NF, JM, SUB, N), F32),
            pltpu.VMEM((TERMS, JM, SUB, N), F32),
            pltpu.VMEM((NF, N, N), F32),
            pltpu.VMEM((NF * KR * SUB, N), F32),
            pltpu.SMEM((1, N), jnp.int32),
            pltpu.VMEM((4, 4 * N), jnp.int32),
            pltpu.VMEM((5, 4, N), jnp.int32),
            pltpu.SemaphoreType.DMA((3,)),
            pltpu.SemaphoreType.DMA((3,)),
            pltpu.SemaphoreType.DMA((2,)),
            pltpu.SemaphoreType.DMA((2,)),
            pltpu.SemaphoreType.DMA((2,)),
            pltpu.SemaphoreType.DMA((5,)),
        ],
        compiler_params=pltpu.CompilerParams(vmem_limit_bytes=VMEM_ALL),
        cost_estimate=pl.CostEstimate(flops=60_000_000, bytes_accessed=1_600_000, transcendentals=0),
        name=name,
    )(mig, fields, mask, *more)


def finish_kernel(
    near_hbm, mig_hbm, halo_hbm, cols_ref, rows_ref, low_ref, high_ref, out_ref,
    near_ref, mig_ref, halo_ref, wide, own, flip, cwork, rwork, terms, stage, isem, ssem, osem, nsem,
):
    fetch_halo = pltpu.make_async_copy(halo_hbm, halo_ref, nsem.at[0])
    fetch_near = pltpu.make_async_copy(near_hbm, near_ref, nsem.at[1])
    fetch_mig = pltpu.make_async_copy(mig_hbm, mig_ref, nsem.at[2])
    fetch_halo.start()
    fetch_near.start()
    fetch_mig.start()
    fetch_cols = pltpu.make_async_copy(cols_ref, own, isem.at[0])
    fetch_rows = pltpu.make_async_copy(rows_ref, rwork.at[0], isem.at[1])
    fetch_cols.start()
    fetch_rows.start()
    fetch_low = pltpu.make_async_copy(low_ref, stage.at[0:2], ssem.at[0])
    fetch_high = pltpu.make_async_copy(high_ref, stage.at[2:4], ssem.at[1])
    fetch_low.start()
    fetch_high.start()
    lane_all = lanes_of((N, N))
    fetch_halo.wait()

    def halo_columns(f, carry):
        halo_lane = ((lane_all & 31) - 12 + 8 * f) & (N - 1)
        for i in range(4):
            moved = lane_pick(halo_ref[pl.ds(i, N, stride=4), :], halo_lane)
            acc = moved if i == 0 else jnp.where(lane_all >= 32 * i, moved, acc)
        wide[f, 4 : 4 + N, :] = acc
        return carry

    lax.fori_loop(0, NF, halo_columns, 0)
    fetch_cols.wait()
    fetch_rows.wait()

    def own_columns(f, carry):
        inside = ((lane_all & 31) >= 12) & ((lane_all & 31) < 20)
        wide[f, 4 : 4 + N, :] = jnp.where(inside, wide[f, 4 : 4 + N, :], own[f])
        return carry

    lax.fori_loop(0, NF, own_columns, 0)
    lane4 = lanes_of((4, N))
    ends_lane = jnp.where((lane4 & 31) < 16, (lane4 & 31) - 12, (lane4 & 31) - 20) & (N - 1)
    flip[N:136, :] = jnp.zeros((8, N), F32)

    def halo_rows(i, carry):
        flip[0:N, :] = jnp.transpose(halo_ref[pl.ds(i, N, stride=4), :])
        here = lane4 // 32 == i
        for f in range(NF):
            for high in range(2):
                if high:
                    edge = flip[SOUTH + 4 * f : SOUTH + 4 * f + 4, :]
                    corner = flip[SOUTH_CORNER + 3 * f : SOUTH_CORNER + 3 * f + 4, :]
                else:
                    shift = 0 if f < 5 else 1
                    edge = flip[NORTH + 4 * f - shift : NORTH + 4 * f - shift + 4, :]
                    start = NORTH_CORNER - 1 + 3 * f if f < 5 else NORTH_CORNER + 13
                    corner = flip[start : start + 4, :]
                ends = jnp.where(
                    ((lane4 & 31) >= 12) & ((lane4 & 31) < 20), lane_pick(corner, ends_lane), lane_pick(edge, ends_lane)
                )
                at = 132 if high else 0
                wide[f, at : at + 4, :] = jnp.where(here, ends, wide[f, at : at + 4, :])
                k0 = 8 if high else 0
                for r in range(4):
                    rwork[0, f, k0 + r, pl.ds(2 * i + high, 1), :] = edge[r : r + 1, :]
        return carry

    lax.fori_loop(0, 4, halo_rows, 0)

    def arrange(f, carry):
        for j in range(JC):
            cwork[0, f, j] = wide[f, pl.ds(j, SUB, stride=JC), :]
        return carry

    lax.fori_loop(0, NF, arrange, 0)

    fetch_near.wait()
    fetch_mig.wait()
    dev = lax.axis_index("curve")
    moving = mig_ref[0, dev]
    before = (dev + N - 1) & (N - 1)
    lane = lanes_of((SUB, N))
    sub = subs_of((SUB, N))
    group = lane // 32

    lacks = []
    for i in range(4):
        patch = 4 * dev + slot_of(i, moving) if i < 3 else 4 * before + mig_ref[0, before]
        lacks.append([(near_ref[k, patch] < 0).astype(jnp.int32) for k in range(4)])

    def by_group(k):
        v = jnp.zeros((SUB, N), jnp.int32)
        for i in range(4):
            v = jnp.where(group == i, lacks[i][k], v)
        return v != 0

    in_group = lane & 31
    no_west, no_east, no_south, no_north = (by_group(k) for k in range(4))
    source = jnp.where(no_west & ((in_group == 18) | (in_group == 19)), lane - in_group + 20, lane)
    source = jnp.where(no_east & ((in_group == 12) | (in_group == 13)), lane - in_group + 11, source)
    low_fix = no_south & (sub == 0)
    high_fix = no_north & (sub == 7)
    row_flag = jnp.zeros((SUB, N), jnp.int32)
    for i in range(4):
        row_flag = jnp.where(sub == 2 * i, lacks[i][2], row_flag)
        row_flag = jnp.where(sub == 2 * i + 1, lacks[i][3], row_flag)
    row_low = (row_flag != 0) & ((sub & 1) == 0)
    row_high = (row_flag != 0) & ((sub & 1) == 1)

    def edge(f, carry):
        for j in range(JC):
            cwork[0, f, j] = lane_pick(cwork[0, f, j], source)
        for j in (2, 3):
            cwork[0, f, j] = jnp.where(low_fix, cwork[0, f, 4], cwork[0, f, j])
        for j in (13, 14):
            cwork[0, f, j] = jnp.where(high_fix, cwork[0, f, 12], cwork[0, f, j])
        return carry

    def step(k, carry):
        @pl.when(k == 0)
        def _():
            lax.fori_loop(0, NF, edge, 0)
            for j in range(JC):
                cwork[1, 5, j] = cwork[0, 5, j]

        @pl.when(k == 2)
        def _():
            lax.fori_loop(0, 5, edge, 0)

        a, b = k & 1, 1 - (k & 1)

        def load(j, f):
            return cwork[a, f, j]

        def store(j, f, value):
            cwork[b, f, j] = value

        advance_tiles(load, store, terms, 0, JC, JC)
        return carry

    lax.fori_loop(0, 4, step, 0)

    def row_edges(fields):
        for f in fields:
            for k in (2, 3):
                rwork[0, f, k] = jnp.where(row_low, rwork[0, f, 4], rwork[0, f, k])
            for k in (8, 9):
                rwork[0, f, k] = jnp.where(row_high, rwork[0, f, 7], rwork[0, f, k])

    row_edges((5,))
    for j in range(KR):
        rwork[1, 5, j] = rwork[0, 5, j]

    def row_step(k, carry):
        @pl.when((k & 1) == 0)
        def _():
            row_edges(range(5))

        a, b = k & 1, 1 - (k & 1)

        def load(j, f):
            return rwork[a, f, j]

        def store(j, f, value):
            rwork[b, f, j] = value

        @pl.when(k < 2)
        def _():
            advance_tiles(load, store, terms, 1, 11, KR)

        @pl.when(k >= 2)
        def _():
            advance_tiles(load, store, terms, 3, 9, KR)

        return carry

    lax.fori_loop(0, 4, row_step, 0)

    def restore(f, carry):
        for j in range(JC):
            wide[f, pl.ds(j, SUB, stride=JC), :] = cwork[0, f, j]
        return carry

    lax.fori_loop(0, 5, restore, 0)
    fetch_low.wait()
    fetch_high.wait()

    def put_out(i):
        slot = jnp.where(i == 3, moving, i + (moving <= i).astype(jnp.int32))
        return pltpu.make_async_copy(stage.at[i], out_ref.at[slot], osem.at[i])

    def merge(i, carry):
        strip_lane = (jnp.where(lane_all < 64, lane_all + 20, lane_all - 116) + 32 * i) & (N - 1)
        for f in range(5):
            for r in range(4):
                stage[i, f, r : r + 1, :] = rwork[0, f, 4 + r, pl.ds(2 * i, 1), :]
                stage[i, f, 124 + r : 125 + r, :] = rwork[0, f, 4 + r, pl.ds(2 * i + 1, 1), :]
            strip = wide[f, 4 : 4 + N, :]
            stage[i, f] = jnp.where((lane_all < 4) | (lane_all >= 124), lane_pick(strip, strip_lane), stage[i, f])
        put_out(i).start()
        return carry

    lax.fori_loop(0, 4, merge, 0)
    for i in range(4):
        put_out(i).wait()


def finish(near, mig, halo, cols, rows, low, high):
    hbm = pl.BlockSpec(memory_space=pl.ANY)
    return pl.pallas_call(
        finish_kernel,
        out_shape=jax.ShapeDtypeStruct((4, NF, N, N), F32),
        in_specs=[hbm] * 7,
        out_specs=hbm,
        scratch_shapes=[
            pltpu.SMEM((4, 4 * N), jnp.int32),
            pltpu.SMEM((1, N), jnp.int32),
            pltpu.VMEM((4 * N, N), F32),
            pltpu.VMEM((NF, 136, N), F32),
            pltpu.VMEM((NF, N, N), F32),
            pltpu.VMEM((136, N), F32),
            pltpu.VMEM((2, NF, JC, SUB, N), F32),
            pltpu.VMEM((2, NF, KR, SUB, N), F32),
            pltpu.VMEM((TERMS, JC, SUB, N), F32),
            pltpu.VMEM((4, NF, N, N), F32),
            pltpu.SemaphoreType.DMA((2,)),
            pltpu.SemaphoreType.DMA((2,)),
            pltpu.SemaphoreType.DMA((4,)),
            pltpu.SemaphoreType.DMA((3,)),
        ],
        compiler_params=pltpu.CompilerParams(vmem_limit_bytes=VMEM_ALL),
        cost_estimate=pl.CostEstimate(flops=30_000_000, bytes_accessed=3_000_000, transcendentals=0),
        name="finish",
    )(near, mig, halo, cols, rows, low, high)


def swap(rows):
    return lax.all_to_all(rows.reshape(N, 4, N), "curve", 0, 0, tiled=True).reshape(4 * N, N)


def shards(fields, wet_mask, neighbors, migration):
    near, mig = neighbors.T, migration.T
    owners = lax.axis_size("curve")
    messages, leaving = make_messages(mig, fields, wet_mask)
    spread = swap(messages)
    low, cols, rows, leaving, *tables = interiors(False, "first", mig, fields, wet_mask, near, leaving)
    patch = lax.ppermute(leaving, "curve", [(d, (d + 1) % owners) for d in range(owners)])
    tables = [table.reshape(4 * N) for table in tables]
    halo = swap(route(tables, migration.reshape(N), spread))
    high, cols, rows = interiors(True, "second", mig, fields, wet_mask, patch, cols, rows)
    return finish(near, mig, halo, cols, rows.reshape(NF, KR, SUB, N), low, high)


def solution(mesh):
    placed = (P("curve", None, None, None), P("curve", None, None), P(), P())
    return jax.shard_map(
        shards, mesh=mesh, in_specs=placed, out_specs=P("curve", None, None, None), check_vma=False
    )
```

```python
import jax
import jax.numpy as jnp
from jax import lax
from jax.experimental import pallas as pl
from jax.experimental.pallas import tpu as pltpu
from jax.sharding import PartitionSpec as P

GRAVITY = 9.81
TIME_STEP = 0.04
DRY_EPS = 0.01
CAPACITY = 0.02
EROSION = 0.5
SETTLING = 0.2
POROSITY = 0.4

F32 = jnp.float32
NF = 6
N = 128
SUB = 8
JM = 16
JC = 17
KR = 12
VMEM_ALL = 67_043_328
SHIFT = 16
CORNER = 3

NORTH, SOUTH, NORTH_CORNER, SOUTH_CORNER = 48, 71, 94, 111


def lanes_of(shape):
    return lax.broadcasted_iota(jnp.int32, shape, 1)


def subs_of(shape):
    return lax.broadcasted_iota(jnp.int32, shape, 0)


def lane_pick(v, index):
    return jnp.take_along_axis(v, index, axis=1, mode="promise_in_bounds")


def to_the_east(v):
    return pltpu.roll(v, N - 1, 1)


def to_the_west(v):
    return pltpu.roll(v, 1, 1)


def root(x):
    return x * lax.rsqrt(x)


def root_from_zero(x):
    return root(jnp.maximum(x, 1e-30))


def cell_terms(h, qx, qy, m):
    hp = jnp.maximum(h, 0.0)
    h2 = h * h
    a = h / (h2 + DRY_EPS)
    u, v, s = qx * a, qy * a, m * a
    r = root(hp + 0.01)
    half = (0.5 * GRAVITY) * h2
    return dict(
        h=h, hp=hp, qx=qx, qy=qy, m=m, r=r, ru=r * u, rv=r * v, rs=r * s,
        fxx=qx * u + half, fxy=qx * v, fyy=qy * v + half, fxs=qx * s, fys=qy * s,
    )


ROLLED_X = ("h", "qx", "qy", "m", "r", "ru", "rv", "rs", "fxx", "fxy", "fxs")


def face_twice(L, R, along_x):
    qn, qt, rn, rt, fn, fs = (
        ("qx", "qy", "ru", "rv", "fxx", "fxs") if along_x else ("qy", "qx", "rv", "ru", "fyy", "fys")
    )
    c = root_from_zero((0.5 * GRAVITY) * (L["hp"] + R["hp"])) + 0.1
    iw, ic2 = 1.0 / (L["r"] + R["r"]), 1.0 / (c + c)
    U = (L[rn] + R[rn]) * iw
    W = (L[rt] + R[rt]) * iw
    S = (L["rs"] + R["rs"]) * iw
    dh = R["h"] - L["h"]
    dn = R[qn] - L[qn]
    dt = R[qt] - L[qt]
    dm = R["m"] - L["m"]
    up, um = U + c, U - c
    p1 = jnp.abs(um) * ((up * dh - dn) * ic2)
    p3 = jnp.abs(up) * ((dn - um * dh) * ic2)
    mid = jnp.abs(U)
    b = p1 + p3
    f_h = (L[qn] + R[qn]) - b
    f_n = (L[fn] + R[fn]) - (p1 * um + p3 * up)
    e = b - mid * dh
    f_t = (L["fxy"] + R["fxy"]) - (W * e + mid * dt)
    f_s = (L[fs] + R[fs]) - (S * e + mid * dm)
    return f_h, f_n, f_t, f_s


def update(C, bed, bed_e, bed_w, bed_n, bed_s, fric, dx, fyn, fys):
    k = 0.5 * TIME_STEP
    h = C["h"]
    slope = (TIME_STEP * GRAVITY * 0.5) * h
    nh = h - k * (dx[0] + (fyn[0] - fys[0]))
    nx = C["qx"] - k * (dx[1] + (fyn[2] - fys[2])) - slope * (bed_e - bed_w)
    ny = C["qy"] - k * (dx[2] + (fyn[1] - fys[1])) - slope * (bed_n - bed_s)
    nm = C["m"] - k * (dx[3] + (fyn[3] - fys[3]))
    a = nh / (nh * nh + DRY_EPS)
    vx, vy = nx * a, ny * a
    speed2 = vx * vx + vy * vy
    speed = root_from_zero(speed2)
    depth = jnp.maximum(nh, 0.0) + 0.1
    factor = depth / (depth + (TIME_STEP * fric) * speed)
    conc = nm * a
    net = EROSION * jnp.maximum(CAPACITY * speed2 - conc, 0.0) - SETTLING * conc
    nm = nm + TIME_STEP * net
    nb = bed - (TIME_STEP / (1.0 - POROSITY)) * net
    return nh, nx * factor, ny * factor, nm, nb


KEPT = ("r", "ru", "rv", "rs", "fxy", "fyy", "fys", "fxx", "fxs")
FLUX = len(KEPT)
MOVED = FLUX + 4
TERMS = MOVED + len(ROLLED_X)


def x_terms(load, terms, j, faces):
    cur = cell_terms(*(load(j, f) for f in range(4)))
    for n, key in enumerate(KEPT):
        terms[n, j] = cur[key]
    if faces:
        for n, key in enumerate(ROLLED_X):
            terms[MOVED + n, j] = to_the_east(cur[key])


def x_faces(load, terms, j):
    L = {key: load(j, f) for f, key in enumerate(("h", "qx", "qy", "m"))}
    for n, key in enumerate(KEPT):
        L[key] = terms[n, j]
    R = {key: terms[MOVED + n, j] for n, key in enumerate(ROLLED_X)}
    for C in (L, R):
        C["hp"] = jnp.maximum(C["h"], 0.0)
    east = face_twice(L, R, True)
    for n in range(4):
        terms[FLUX + n, j] = east[n]


def y_pass(load, store, terms, lo, hi, last):
    wraps = lo == 0

    def around(j, get):
        if j < 0:
            return pltpu.roll(get(last - 1), 1, 0)
        if j == last:
            return pltpu.roll(get(0), SUB - 1, 0)
        return get(j)

    def cell(j):
        C = {key: around(j, lambda t: load(t, f)) for f, key in enumerate(("h", "qx", "qy", "m"))}
        for n, key in enumerate(KEPT):
            C[key] = around(j, lambda t: terms[n, t])
        C["hp"] = jnp.maximum(C["h"], 0.0)
        return C

    if wraps:
        top = face_twice(cell(last - 1), cell(last), False)
        south = tuple(pltpu.roll(x, 1, 0) for x in top)
    else:
        south = face_twice(cell(lo - 1), cell(lo), False)
    cur = cell(lo)
    for j in range(lo, hi):
        if wraps and j == last - 1:
            nxt, north = None, top
        else:
            nxt = cell(j + 1)
            north = face_twice(cur, nxt, False)
        bed = load(j, 4)
        dx = tuple(terms[FLUX + n, j] - to_the_west(terms[FLUX + n, j]) for n in range(4))
        bed_n, bed_s = (around(t, lambda t: load(t, 4)) for t in (j + 1, j - 1))
        new = update(
            cur, bed, to_the_east(bed), to_the_west(bed), bed_n, bed_s, load(j, 5), dx, north, south,
        )
        for f in range(5):
            store(j, f, new[f])
        south = north
        cur = cell(j + 1) if j + 1 < hi else None


def advance_tiles(load, store, terms, lo, hi, last):
    span = range(last) if lo == 0 else range(lo - 1, hi + 1)
    for j in span:
        x_terms(load, terms, j, lo <= j < hi)
    for j in range(lo, hi):
        x_faces(load, terms, j)
    y_pass(load, store, terms, lo, hi, last)


def slot_of(i, moving):
    if i == 3:
        return moving
    return i + (moving <= i).astype(jnp.int32)


def message_kernel(mig_hbm, fields_ref, mask_ref, out_ref, leave_ref, fbuf, mbuf, tbuf, mig_ref, fsem, msem, gsem, lsem):
    def fetches(t):
        return (
            pltpu.make_async_copy(fields_ref.at[t], fbuf.at[t], fsem.at[t]),
            pltpu.make_async_copy(mask_ref.at[t], mbuf.at[t], msem.at[t]),
        )

    for t in range(4):
        for cp in fetches(t):
            cp.start()
    fetch = pltpu.make_async_copy(mig_hbm, mig_ref, gsem)
    fetch.start()
    lane = lanes_of((N, N))
    edge_lane = (lane & 3) + jnp.where((lane & 4) != 0, 124, 0)

    def body(t, carry):
        for cp in fetches(t):
            cp.wait()
        wet = mbuf[t].astype(F32)
        for f in range(4):
            fbuf[t, f] = fbuf[t, f] * wet
        for f in range(NF):
            depth = 4 if f < 5 else 3
            low = 4 - depth
            tbuf[NORTH + 4 * f : NORTH + 4 * f + depth, :] = fbuf[t, f, 124 + low : 128, :]
            tbuf[SOUTH + 4 * f : SOUTH + 4 * f + depth, :] = fbuf[t, f, 0:depth, :]
            tbuf[NORTH_CORNER + 3 * f : NORTH_CORNER + 3 * f + depth - 1, :] = fbuf[t, f, 129 - depth : 128, :]
            tbuf[SOUTH_CORNER + 3 * f : SOUTH_CORNER + 3 * f + depth - 1, :] = fbuf[t, f, 0 : depth - 1, :]
        acc = jnp.transpose(tbuf[...])
        for f in range(NF):
            v = fbuf[t, f]
            acc = jnp.where((lane >= 8 * f) & (lane < 8 * f + 8), lane_pick(v, edge_lane), acc)
        out_ref[pl.ds(t, N - SHIFT, stride=4), :] = acc[SHIFT:]
        out_ref[pl.ds(t + 4 * (N - SHIFT), SHIFT, stride=4), :] = acc[:SHIFT]

        @pl.when(t == 0)
        def _():
            fetch.wait()

        @pl.when(mig_ref[0, lax.axis_index("curve")] == t)
        def _():
            pltpu.make_async_copy(fbuf.at[t], leave_ref, lsem).start()

        return carry

    lax.fori_loop(0, 4, body, 0)
    pltpu.make_async_copy(fbuf.at[0], leave_ref, lsem).wait()


def make_messages(mig, fields, mask):
    return pl.pallas_call(
        message_kernel,
        out_shape=(
            jax.ShapeDtypeStruct((4 * N, N), F32),
            jax.ShapeDtypeStruct((NF, N, N), F32),
        ),
        in_specs=[pl.BlockSpec(memory_space=pl.ANY)] * 3,
        out_specs=(pl.BlockSpec(memory_space=pltpu.VMEM), pl.BlockSpec(memory_space=pl.ANY)),
        scratch_shapes=[
            pltpu.VMEM((4, NF, N, N), F32),
            pltpu.VMEM((4, N, N), jnp.int32),
            pltpu.VMEM((N, N), F32),
            pltpu.SMEM((1, N), jnp.int32),
            pltpu.SemaphoreType.DMA((4,)),
            pltpu.SemaphoreType.DMA((4,)),
            pltpu.SemaphoreType.DMA,
            pltpu.SemaphoreType.DMA,
        ],
        compiler_params=pltpu.CompilerParams(vmem_limit_bytes=VMEM_ALL),
        cost_estimate=pl.CostEstimate(flops=2_000_000, bytes_accessed=3_000_000, transcendentals=0),
        name="messages",
    )(mig, fields, mask)


def route_kernel(w_hbm, e_hbm, s_hbm, n_hbm, side_hbm, mig_hbm, rows_hbm, out_ref, w_ref, e_ref, s_ref, n_ref, side_ref, mig_ref, table, picked, sem, osem):
    fetches = tuple(
        pltpu.make_async_copy(a, b, sem.at[k])
        for k, (a, b) in enumerate(
            (
                (w_hbm, w_ref), (e_hbm, e_ref), (s_hbm, s_ref), (n_hbm, n_ref),
                (side_hbm, side_ref), (mig_hbm, mig_ref), (rows_hbm, table),
            )
        )
    )
    for cp in fetches:
        cp.start()
    position = (lax.axis_index("curve") + SHIFT) & (N - 1)
    lane = lanes_of((1, N))
    from_west = (lane < NORTH) & ((lane & 4) != 0)
    from_east = (lane < NORTH) & ((lane & 4) == 0)
    from_south = lane < SOUTH
    from_north = lane < NORTH_CORNER
    from_low = lane < SOUTH_CORNER
    for cp in fetches:
        cp.wait()

    def pick(p, place, corners):
        s, n = s_ref[p], n_ref[p]
        row = table[pl.ds(n, 1), :]
        if corners:
            far = jnp.where(from_low, table[pl.ds(side_ref[s], 1), :], table[pl.ds(side_ref[n], 1), :])
            row = jnp.where(from_north, row, far)
        row = jnp.where(from_south, table[pl.ds(s, 1), :], row)
        row = jnp.where(from_east, table[pl.ds(e_ref[p], 1), :], row)
        row = jnp.where(from_west, table[pl.ds(w_ref[p], 1), :], row)
        picked[pl.ds(place, 1), :] = row

    def put(c):
        span = pl.ds(N * c, N)
        return pltpu.make_async_copy(picked.at[span], out_ref.at[span], osem.at[c])

    def run(corners):
        def body(d, carry):
            moving = mig_ref[d]
            first = 4 * d
            for i in range(3):
                pick(jnp.where(moving <= i, first + (i + 1), first + i), first + i, corners)
            pick(first + moving, first + 7, corners)
            return carry

        def chunk(c, carry):
            def four(g, inner):
                for u in range(4):
                    body(32 * c + 4 * g + u, inner)
                return inner

            lax.fori_loop(0, 8, four, 0)
            put(c).start()
            return carry

        pick(4 * (N - 1) + mig_ref[N - 1], 3, corners)
        lax.fori_loop(0, 4, chunk, 0)

    at_corner = (position < CORNER) | (position >= N - CORNER)

    @pl.when(at_corner)
    def _():
        run(True)

    @pl.when(jnp.logical_not(at_corner))
    def _():
        run(False)

    for c in range(4):
        put(c).wait()


def route(tables, mig, rows):
    hbm = pl.BlockSpec(memory_space=pl.ANY)
    return pl.pallas_call(
        route_kernel,
        out_shape=jax.ShapeDtypeStruct((4 * N, N), F32),
        in_specs=[hbm] * 7,
        out_specs=hbm,
        scratch_shapes=[
            *(pltpu.SMEM((4 * N,), jnp.int32) for _ in range(5)),
            pltpu.SMEM((N,), jnp.int32),
            pltpu.VMEM((4 * N, N), F32),
            pltpu.VMEM((4 * N + SUB, N), F32),
            pltpu.SemaphoreType.DMA((7,)),
            pltpu.SemaphoreType.DMA((4,)),
        ],
        compiler_params=pltpu.CompilerParams(vmem_limit_bytes=VMEM_ALL),
        cost_estimate=pl.CostEstimate(flops=2_000_000, bytes_accessed=2_000_000, transcendentals=0),
        name="route",
    )(*tables, mig, rows)


def own_strips(patch, i, lane, cols, rows):
    at = lane - 32 * i
    inside = (at >= 4) & (at < 28)
    source = jnp.where(at < 16, at + 116, at - 20) & (N - 1)
    for f in range(NF):
        v = patch[f]
        cols[f] = jnp.where(inside, lane_pick(v, source), cols[f])
        rows[pl.ds((f * KR + 4) * SUB + 2 * i, 8, stride=SUB), :] = patch[f, 0:8, :]
        rows[pl.ds((f * KR) * SUB + 2 * i + 1, 8, stride=SUB), :] = patch[f, 120:128, :]


def interior(patch, work, terms):
    for f in range(NF):
        for j in range(JM):
            work[0, f, j] = patch[f, pl.ds(j, SUB, stride=JM), :]
            if f == 5:
                work[1, f, j] = work[0, f, j]

    def step(k, carry):
        a, b = k & 1, 1 - (k & 1)

        def load(j, f):
            return work[a, f, j]

        def store(j, f, value):
            work[b, f, j] = value

        advance_tiles(load, store, terms, 0, JM, JM)
        return carry

    lax.fori_loop(0, 4, step, 0)
    for f in range(5):
        for j in range(JM):
            patch[f, pl.ds(j, SUB, stride=JM), :] = work[0, f, j]


def interior_kernel(arrival, refs):
    mig_hbm, fields_ref, mask_ref = refs[:3]
    if arrival:
        come_ref, cols_in, rows_in = refs[3:6]
        out_ref, cols_ref, rows_ref = refs[6:9]
    else:
        near_ref, leave_ref = refs[3:5]
        out_ref, cols_ref, rows_ref, passed_ref = refs[5:9]
        known_refs = refs[9:14]
        del leave_ref, passed_ref
    fbuf, mbuf, work, terms, cols, rows, mig_ref, near_buf, known, fsem, msem, csem, osem, gsem, ksem = refs[-15:]
    first = 2 if arrival else 0
    slots = 2 if arrival else 3
    come = slots

    def fetches(n):
        return (
            pltpu.make_async_copy(fields_ref.at[first + n], fbuf.at[n], fsem.at[n]),
            pltpu.make_async_copy(mask_ref.at[first + n], mbuf.at[n], msem.at[n]),
        )

    fetch_mig = pltpu.make_async_copy(mig_hbm, mig_ref, gsem.at[0])
    fetch_mig.start()
    for n in range(slots):
        for cp in fetches(n):
            cp.start()
    if arrival:
        given = (
            pltpu.make_async_copy(cols_in, cols, csem.at[0]),
            pltpu.make_async_copy(rows_in, rows, csem.at[1]),
            pltpu.make_async_copy(come_ref, fbuf.at[come], fsem.at[come]),
        )
        for cp in given:
            cp.start()
    else:
        fetch_near = pltpu.make_async_copy(near_ref, near_buf, gsem.at[1])
        fetch_near.start()
        cols[...] = jnp.zeros(cols.shape, F32)
        rows[...] = jnp.zeros(rows.shape, F32)
    fetch_mig.wait()
    moving = mig_ref[0, lax.axis_index("curve")]
    if not arrival:
        fetch_near.wait()
        for c in range(4):
            part = [jnp.maximum(near_buf[k : k + 1, c * N : (c + 1) * N], 0) for k in range(4)]
            part.append(jnp.where(((lax.axis_index("curve") + SHIFT) & (N - 1)) < N // 2, part[1], part[0]))
            for k in range(5):
                known[k, c : c + 1, :] = part[k]
        give = [pltpu.make_async_copy(known.at[k], known_refs[k], ksem.at[k]) for k in range(5)]
        for cp in give:
            cp.start()
    lane = lanes_of((N, N))

    def mask_patch(n):
        wet = mbuf[n].astype(F32)
        for f in range(4):
            fbuf[n, f] = fbuf[n, f] * wet

    def place_of(n):
        place = n + (moving <= first + n).astype(jnp.int32)
        return jnp.where(n == 1, come, place) if arrival else place

    def run(n, carry):
        place = place_of(n)

        @pl.when(n == 0)
        def _():
            for t in range(slots):
                for cp in fetches(t):
                    cp.wait()
            if arrival:
                for cp in given:
                    cp.wait()

        if arrival:

            @pl.when(n == 0)
            def _():
                mask_patch(place)
        else:
            mask_patch(place)
        patch = fbuf.at[place]
        own_strips(patch, first + n, lane, cols, rows)
        interior(patch, work, terms)
        pltpu.make_async_copy(patch, out_ref.at[n], osem.at[n]).start()
        return carry

    lax.fori_loop(0, 2, run, 0)
    last = (
        pltpu.make_async_copy(cols, cols_ref, csem.at[0]),
        pltpu.make_async_copy(rows, rows_ref, csem.at[1]),
    )
    for cp in last:
        cp.start()
    for n in range(2):
        pltpu.make_async_copy(fbuf.at[n], out_ref.at[n], osem.at[n]).wait()
    for cp in last:
        cp.wait()
    if not arrival:
        for cp in give:
            cp.wait()


def interiors(arrival, name, mig, fields, mask, *more):
    hbm = pl.BlockSpec(memory_space=pl.ANY)

    def kernel(*refs):
        interior_kernel(arrival, refs)

    return pl.pallas_call(
        kernel,
        out_shape=(
            jax.ShapeDtypeStruct((2, NF, N, N), F32),
            jax.ShapeDtypeStruct((NF, N, N), F32),
            jax.ShapeDtypeStruct((NF * KR * SUB, N), F32),
        )
        + (() if arrival else (jax.ShapeDtypeStruct((NF, N, N), F32),) + (jax.ShapeDtypeStruct((4, N), jnp.int32),) * 5),
        in_specs=[hbm] * (3 + len(more)),
        out_specs=(hbm,) * (3 if arrival else 9),
        input_output_aliases={} if arrival else {4: 3},
        scratch_shapes=[
            pltpu.VMEM((3, NF, N, N), F32),
            pltpu.VMEM((3, N, N), jnp.int32),
            pltpu.VMEM((2, NF, JM, SUB, N), F32),
            pltpu.VMEM((TERMS, JM, SUB, N), F32),
            pltpu.VMEM((NF, N, N), F32),
            pltpu.VMEM((NF * KR * SUB, N), F32),
            pltpu.SMEM((1, N), jnp.int32),
            pltpu.VMEM((4, 4 * N), jnp.int32),
            pltpu.VMEM((5, 4, N), jnp.int32),
            pltpu.SemaphoreType.DMA((3,)),
            pltpu.SemaphoreType.DMA((3,)),
            pltpu.SemaphoreType.DMA((2,)),
            pltpu.SemaphoreType.DMA((2,)),
            pltpu.SemaphoreType.DMA((2,)),
            pltpu.SemaphoreType.DMA((5,)),
        ],
        compiler_params=pltpu.CompilerParams(vmem_limit_bytes=VMEM_ALL),
        cost_estimate=pl.CostEstimate(flops=60_000_000, bytes_accessed=1_600_000, transcendentals=0),
        name=name,
    )(mig, fields, mask, *more)


def finish_kernel(
    near_hbm, mig_hbm, halo_hbm, cols_ref, rows_ref, low_ref, high_ref, out_ref,
    near_ref, mig_ref, halo_ref, wide, own, flip, cwork, rwork, terms, stage, isem, ssem, osem, nsem,
):
    turn = 4 * SHIFT
    fetch_halo = (
        pltpu.make_async_copy(halo_hbm.at[pl.ds(4 * N - turn, turn)], halo_ref.at[pl.ds(0, turn)], nsem.at[0]),
        pltpu.make_async_copy(halo_hbm.at[pl.ds(0, 4 * N - turn)], halo_ref.at[pl.ds(turn, 4 * N - turn)], nsem.at[3]),
    )
    fetch_near = pltpu.make_async_copy(near_hbm, near_ref, nsem.at[1])
    fetch_mig = pltpu.make_async_copy(mig_hbm, mig_ref, nsem.at[2])
    for cp in fetch_halo:
        cp.start()
    fetch_near.start()
    fetch_mig.start()
    fetch_cols = pltpu.make_async_copy(cols_ref, own, isem.at[0])
    fetch_rows = pltpu.make_async_copy(rows_ref, rwork.at[0], isem.at[1])
    fetch_cols.start()
    fetch_rows.start()
    fetch_low = pltpu.make_async_copy(low_ref, stage.at[0:2], ssem.at[0])
    fetch_high = pltpu.make_async_copy(high_ref, stage.at[2:4], ssem.at[1])
    fetch_low.start()
    fetch_high.start()
    lane_all = lanes_of((N, N))
    for cp in fetch_halo:
        cp.wait()

    def halo_columns(f, carry):
        halo_lane = ((lane_all & 31) - 12 + 8 * f) & (N - 1)
        for i in range(4):
            moved = lane_pick(halo_ref[pl.ds(i, N, stride=4), :], halo_lane)
            acc = moved if i == 0 else jnp.where(lane_all >= 32 * i, moved, acc)
        wide[f, 4 : 4 + N, :] = acc
        return carry

    lax.fori_loop(0, NF, halo_columns, 0)
    fetch_cols.wait()
    fetch_rows.wait()

    def own_columns(f, carry):
        inside = ((lane_all & 31) >= 12) & ((lane_all & 31) < 20)
        wide[f, 4 : 4 + N, :] = jnp.where(inside, wide[f, 4 : 4 + N, :], own[f])
        return carry

    lax.fori_loop(0, NF, own_columns, 0)
    lane4 = lanes_of((4, N))
    ends_lane = jnp.where((lane4 & 31) < 16, (lane4 & 31) - 12, (lane4 & 31) - 20) & (N - 1)
    flip[N:136, :] = jnp.zeros((8, N), F32)

    def halo_rows(i, carry):
        flip[0:N, :] = jnp.transpose(halo_ref[pl.ds(i, N, stride=4), :])
        here = lane4 // 32 == i
        for f in range(NF):
            for high in range(2):
                if high:
                    edge = flip[SOUTH + 4 * f : SOUTH + 4 * f + 4, :]
                    corner = flip[SOUTH_CORNER + 3 * f : SOUTH_CORNER + 3 * f + 4, :]
                else:
                    shift = 0 if f < 5 else 1
                    edge = flip[NORTH + 4 * f - shift : NORTH + 4 * f - shift + 4, :]
                    start = NORTH_CORNER - 1 + 3 * f if f < 5 else NORTH_CORNER + 13
                    corner = flip[start : start + 4, :]
                ends = jnp.where(
                    ((lane4 & 31) >= 12) & ((lane4 & 31) < 20), lane_pick(corner, ends_lane), lane_pick(edge, ends_lane)
                )
                at = 132 if high else 0
                wide[f, at : at + 4, :] = jnp.where(here, ends, wide[f, at : at + 4, :])
                k0 = 8 if high else 0
                for r in range(4):
                    rwork[0, f, k0 + r, pl.ds(2 * i + high, 1), :] = edge[r : r + 1, :]
        return carry

    lax.fori_loop(0, 4, halo_rows, 0)

    def arrange(f, carry):
        for j in range(JC):
            cwork[0, f, j] = wide[f, pl.ds(j, SUB, stride=JC), :]
        return carry

    lax.fori_loop(0, NF, arrange, 0)

    fetch_near.wait()
    fetch_mig.wait()
    dev = lax.axis_index("curve")
    moving = mig_ref[0, dev]
    before = (dev + N - 1) & (N - 1)
    lane = lanes_of((SUB, N))
    sub = subs_of((SUB, N))
    group = lane // 32

    lacks = []
    for i in range(4):
        patch = 4 * dev + slot_of(i, moving) if i < 3 else 4 * before + mig_ref[0, before]
        lacks.append([(near_ref[k, patch] < 0).astype(jnp.int32) for k in range(4)])

    def by_group(k):
        v = jnp.zeros((SUB, N), jnp.int32)
        for i in range(4):
            v = jnp.where(group == i, lacks[i][k], v)
        return v != 0

    in_group = lane & 31
    no_west, no_east, no_south, no_north = (by_group(k) for k in range(4))
    source = jnp.where(no_west & ((in_group == 18) | (in_group == 19)), lane - in_group + 20, lane)
    source = jnp.where(no_east & ((in_group == 12) | (in_group == 13)), lane - in_group + 11, source)
    low_fix = no_south & (sub == 0)
    high_fix = no_north & (sub == 7)
    row_flag = jnp.zeros((SUB, N), jnp.int32)
    for i in range(4):
        row_flag = jnp.where(sub == 2 * i, lacks[i][2], row_flag)
        row_flag = jnp.where(sub == 2 * i + 1, lacks[i][3], row_flag)
    row_low = (row_flag != 0) & ((sub & 1) == 0)
    row_high = (row_flag != 0) & ((sub & 1) == 1)

    def edge(f, carry):
        for j in range(JC):
            cwork[0, f, j] = lane_pick(cwork[0, f, j], source)
        for j in (2, 3):
            cwork[0, f, j] = jnp.where(low_fix, cwork[0, f, 4], cwork[0, f, j])
        for j in (13, 14):
            cwork[0, f, j] = jnp.where(high_fix, cwork[0, f, 12], cwork[0, f, j])
        return carry

    def step(k, carry):
        @pl.when(k == 0)
        def _():
            lax.fori_loop(0, NF, edge, 0)
            for j in range(JC):
                cwork[1, 5, j] = cwork[0, 5, j]

        @pl.when(k == 2)
        def _():
            lax.fori_loop(0, 5, edge, 0)

        a, b = k & 1, 1 - (k & 1)

        def load(j, f):
            return cwork[a, f, j]

        def store(j, f, value):
            cwork[b, f, j] = value

        advance_tiles(load, store, terms, 0, JC, JC)
        return carry

    lax.fori_loop(0, 4, step, 0)

    def row_edges(fields):
        for f in fields:
            for k in (2, 3):
                rwork[0, f, k] = jnp.where(row_low, rwork[0, f, 4], rwork[0, f, k])
            for k in (8, 9):
                rwork[0, f, k] = jnp.where(row_high, rwork[0, f, 7], rwork[0, f, k])

    row_edges((5,))
    for j in range(KR):
        rwork[1, 5, j] = rwork[0, 5, j]

    def row_step(k, carry):
        @pl.when((k & 1) == 0)
        def _():
            row_edges(range(5))

        a, b = k & 1, 1 - (k & 1)

        def load(j, f):
            return rwork[a, f, j]

        def store(j, f, value):
            rwork[b, f, j] = value

        @pl.when(k < 2)
        def _():
            advance_tiles(load, store, terms, 1, 11, KR)

        @pl.when(k >= 2)
        def _():
            advance_tiles(load, store, terms, 3, 9, KR)

        return carry

    lax.fori_loop(0, 4, row_step, 0)

    def restore(f, carry):
        for j in range(JC):
            wide[f, pl.ds(j, SUB, stride=JC), :] = cwork[0, f, j]
        return carry

    lax.fori_loop(0, 5, restore, 0)
    fetch_low.wait()
    fetch_high.wait()

    def put_out(i):
        slot = jnp.where(i == 3, moving, i + (moving <= i).astype(jnp.int32))
        return pltpu.make_async_copy(stage.at[i], out_ref.at[slot], osem.at[i])

    def merge(i, carry):
        strip_lane = (jnp.where(lane_all < 64, lane_all + 20, lane_all - 116) + 32 * i) & (N - 1)
        for f in range(5):
            for r in range(4):
                stage[i, f, r : r + 1, :] = rwork[0, f, 4 + r, pl.ds(2 * i, 1), :]
                stage[i, f, 124 + r : 125 + r, :] = rwork[0, f, 4 + r, pl.ds(2 * i + 1, 1), :]
            strip = wide[f, 4 : 4 + N, :]
            stage[i, f] = jnp.where((lane_all < 4) | (lane_all >= 124), lane_pick(strip, strip_lane), stage[i, f])
        put_out(i).start()
        return carry

    lax.fori_loop(0, 4, merge, 0)
    for i in range(4):
        put_out(i).wait()


def finish(near, mig, halo, cols, rows, low, high):
    hbm = pl.BlockSpec(memory_space=pl.ANY)
    return pl.pallas_call(
        finish_kernel,
        out_shape=jax.ShapeDtypeStruct((4, NF, N, N), F32),
        in_specs=[hbm] * 7,
        out_specs=hbm,
        scratch_shapes=[
            pltpu.SMEM((4, 4 * N), jnp.int32),
            pltpu.SMEM((1, N), jnp.int32),
            pltpu.VMEM((4 * N, N), F32),
            pltpu.VMEM((NF, 136, N), F32),
            pltpu.VMEM((NF, N, N), F32),
            pltpu.VMEM((136, N), F32),
            pltpu.VMEM((2, NF, JC, SUB, N), F32),
            pltpu.VMEM((2, NF, KR, SUB, N), F32),
            pltpu.VMEM((TERMS, JC, SUB, N), F32),
            pltpu.VMEM((4, NF, N, N), F32),
            pltpu.SemaphoreType.DMA((2,)),
            pltpu.SemaphoreType.DMA((2,)),
            pltpu.SemaphoreType.DMA((4,)),
            pltpu.SemaphoreType.DMA((4,)),
        ],
        compiler_params=pltpu.CompilerParams(vmem_limit_bytes=VMEM_ALL),
        cost_estimate=pl.CostEstimate(flops=30_000_000, bytes_accessed=3_000_000, transcendentals=0),
        name="finish",
    )(near, mig, halo, cols, rows, low, high)


def swap(rows):
    return lax.all_to_all(rows.reshape(N, 4, N), "curve", 0, 0, tiled=True).reshape(4 * N, N)


def shards(fields, wet_mask, neighbors, migration):
    near, mig = neighbors.T, migration.T
    owners = lax.axis_size("curve")
    messages, leaving = make_messages(mig, fields, wet_mask)
    spread = swap(messages)
    low, cols, rows, leaving, *tables = interiors(False, "first", mig, fields, wet_mask, near, leaving)
    patch = lax.ppermute(leaving, "curve", [(d, (d + 1) % owners) for d in range(owners)])
    tables = [table.reshape(4 * N) for table in tables]
    halo = swap(route(tables, migration.reshape(N), spread))
    high, cols, rows = interiors(True, "second", mig, fields, wet_mask, patch, cols, rows)
    return finish(near, mig, halo, cols, rows.reshape(NF, KR, SUB, N), low, high)


def solution(mesh):
    placed = (P("curve", None, None, None), P("curve", None, None), P(), P())
    return jax.shard_map(
        shards, mesh=mesh, in_specs=placed, out_specs=P("curve", None, None, None), check_vma=False
    )
```

```python
import jax
import jax.numpy as jnp
from jax import lax
from jax.experimental import pallas as pl
from jax.experimental.pallas import tpu as pltpu
from jax.sharding import PartitionSpec as P

GRAVITY = 9.81
TIME_STEP = 0.04
DRY_EPS = 0.01
CAPACITY = 0.02
EROSION = 0.5
SETTLING = 0.2
POROSITY = 0.4

F32 = jnp.float32
NF = 6
N = 128
SUB = 8
JM = 16
JC = 17
KR = 12
VMEM_ALL = 67_043_328
SHIFT = 16
CORNER = 3

NORTH, SOUTH, NORTH_CORNER, SOUTH_CORNER = 48, 71, 94, 111


def lanes_of(shape):
    return lax.broadcasted_iota(jnp.int32, shape, 1)


def subs_of(shape):
    return lax.broadcasted_iota(jnp.int32, shape, 0)


def lane_pick(v, index):
    return jnp.take_along_axis(v, index, axis=1, mode="promise_in_bounds")


def to_the_east(v):
    return pltpu.roll(v, N - 1, 1)


def to_the_west(v):
    return pltpu.roll(v, 1, 1)


def root(x):
    return x * lax.rsqrt(x)


def root_from_zero(x):
    return root(jnp.maximum(x, 1e-30))


def celerity_term(h):
    return jnp.maximum((0.5 * GRAVITY) * h, 1e-30)


def cell_terms(h, qx, qy, m):
    hp = jnp.maximum(h, 0.0)
    h2 = h * h
    a = h / (h2 + DRY_EPS)
    u, v, s = qx * a, qy * a, m * a
    r = root(hp + 0.01)
    half = (0.5 * GRAVITY) * h2
    hg = celerity_term(h)
    return dict(
        h=h, hg=hg, qx=qx, qy=qy, m=m, r=r, ru=r * u, rv=r * v, rs=r * s,
        fxx=qx * u + half, fxy=qx * v, fyy=qy * v + half, fxs=qx * s, fys=qy * s,
    )


ROLLED_X = ("h", "qx", "qy", "m", "r", "ru", "rv", "rs", "fxx", "fxy", "fxs")


def face_twice(L, R, along_x):
    qn, qt, rn, rt, fn, fs = (
        ("qx", "qy", "ru", "rv", "fxx", "fxs") if along_x else ("qy", "qx", "rv", "ru", "fyy", "fys")
    )
    c = root(L["hg"] + R["hg"]) + 0.1
    iw, ic2 = 1.0 / (L["r"] + R["r"]), 1.0 / (c + c)
    U = (L[rn] + R[rn]) * iw
    W = (L[rt] + R[rt]) * iw
    S = (L["rs"] + R["rs"]) * iw
    dh = R["h"] - L["h"]
    dn = R[qn] - L[qn]
    dt = R[qt] - L[qt]
    dm = R["m"] - L["m"]
    up, um = U + c, U - c
    p1 = jnp.abs(um) * ((up * dh - dn) * ic2)
    p3 = jnp.abs(up) * ((dn - um * dh) * ic2)
    mid = jnp.abs(U)
    b = p1 + p3
    f_h = (L[qn] + R[qn]) - b
    f_n = (L[fn] + R[fn]) - (p1 * um + p3 * up)
    e = b - mid * dh
    f_t = (L["fxy"] + R["fxy"]) - (W * e + mid * dt)
    f_s = (L[fs] + R[fs]) - (S * e + mid * dm)
    return f_h, f_n, f_t, f_s


def update(C, bed, bed_e, bed_w, bed_n, bed_s, fric, dx, fyn, fys):
    k = 0.5 * TIME_STEP
    h = C["h"]
    slope = (TIME_STEP * GRAVITY * 0.5) * h
    nh = h - k * (dx[0] + (fyn[0] - fys[0]))
    nx = C["qx"] - k * (dx[1] + (fyn[2] - fys[2])) - slope * (bed_e - bed_w)
    ny = C["qy"] - k * (dx[2] + (fyn[1] - fys[1])) - slope * (bed_n - bed_s)
    nm = C["m"] - k * (dx[3] + (fyn[3] - fys[3]))
    a = nh / (nh * nh + DRY_EPS)
    vx, vy = nx * a, ny * a
    speed2 = vx * vx + vy * vy
    speed = root_from_zero(speed2)
    depth = jnp.maximum(nh, 0.0) + 0.1
    factor = depth / (depth + fric * speed)
    conc = nm * a
    gain = jnp.maximum((TIME_STEP * EROSION * CAPACITY) * speed2 - (TIME_STEP * EROSION) * conc, 0.0)
    gain = gain - (TIME_STEP * SETTLING) * conc
    nm = nm + gain
    nb = bed - (1.0 / (1.0 - POROSITY)) * gain
    return nh, nx * factor, ny * factor, nm, nb


KEPT = ("hg", "r", "ru", "rv", "rs", "fxy", "fyy", "fys", "fxx", "fxs")
FLUX = len(KEPT)
MOVED = FLUX + 4
TERMS = MOVED + len(ROLLED_X)


def x_terms(load, terms, j, faces):
    cur = cell_terms(*(load(j, f) for f in range(4)))
    for n, key in enumerate(KEPT):
        terms[n, j] = cur[key]
    if faces:
        for n, key in enumerate(ROLLED_X):
            terms[MOVED + n, j] = to_the_east(cur[key])


def x_faces(load, terms, j):
    L = {key: load(j, f) for f, key in enumerate(("h", "qx", "qy", "m"))}
    for n, key in enumerate(KEPT):
        L[key] = terms[n, j]
    R = {key: terms[MOVED + n, j] for n, key in enumerate(ROLLED_X)}
    R["hg"] = celerity_term(R["h"])
    east = face_twice(L, R, True)
    for n in range(4):
        terms[FLUX + n, j] = east[n]


def y_pass(load, store, terms, lo, hi, last):
    wraps = lo == 0

    def around(j, get):
        if j < 0:
            return pltpu.roll(get(last - 1), 1, 0)
        if j == last:
            return pltpu.roll(get(0), SUB - 1, 0)
        return get(j)

    def cell(j):
        C = {key: around(j, lambda t: load(t, f)) for f, key in enumerate(("h", "qx", "qy", "m"))}
        for n, key in enumerate(KEPT):
            C[key] = around(j, lambda t: terms[n, t])
        return C

    if wraps:
        top = face_twice(cell(last - 1), cell(last), False)
        south = tuple(pltpu.roll(x, 1, 0) for x in top)
    else:
        south = face_twice(cell(lo - 1), cell(lo), False)
    cur = cell(lo)
    for j in range(lo, hi):
        if wraps and j == last - 1:
            nxt, north = None, top
        else:
            nxt = cell(j + 1)
            north = face_twice(cur, nxt, False)
        bed = load(j, 4)
        dx = tuple(terms[FLUX + n, j] - to_the_west(terms[FLUX + n, j]) for n in range(4))
        bed_n, bed_s = (around(t, lambda t: load(t, 4)) for t in (j + 1, j - 1))
        new = update(
            cur, bed, to_the_east(bed), to_the_west(bed), bed_n, bed_s, load(j, 5), dx, north, south,
        )
        for f in range(5):
            store(j, f, new[f])
        south = north
        cur = cell(j + 1) if j + 1 < hi else None


def advance_tiles(load, store, terms, lo, hi, last):
    span = range(last) if lo == 0 else range(lo - 1, hi + 1)
    for j in span:
        x_terms(load, terms, j, lo <= j < hi)
    for j in range(lo, hi):
        x_faces(load, terms, j)
    y_pass(load, store, terms, lo, hi, last)


def slot_of(i, moving):
    if i == 3:
        return moving
    return i + (moving <= i).astype(jnp.int32)


def message_kernel(mig_hbm, fields_ref, mask_ref, out_ref, leave_ref, fbuf, mbuf, tbuf, mig_ref, fsem, msem, gsem, lsem):
    def fetches(t):
        return (
            pltpu.make_async_copy(fields_ref.at[t], fbuf.at[t], fsem.at[t]),
            pltpu.make_async_copy(mask_ref.at[t], mbuf.at[t], msem.at[t]),
        )

    for t in range(4):
        for cp in fetches(t):
            cp.start()
    fetch = pltpu.make_async_copy(mig_hbm, mig_ref, gsem)
    fetch.start()
    lane = lanes_of((N, N))
    edge_lane = (lane & 3) + jnp.where((lane & 4) != 0, 124, 0)

    def body(t, carry):
        for cp in fetches(t):
            cp.wait()
        wet = mbuf[t].astype(F32)
        for f in range(4):
            fbuf[t, f] = fbuf[t, f] * wet
        for f in range(NF):
            depth = 4 if f < 5 else 3
            low = 4 - depth
            tbuf[NORTH + 4 * f : NORTH + 4 * f + depth, :] = fbuf[t, f, 124 + low : 128, :]
            tbuf[SOUTH + 4 * f : SOUTH + 4 * f + depth, :] = fbuf[t, f, 0:depth, :]
            tbuf[NORTH_CORNER + 3 * f : NORTH_CORNER + 3 * f + depth - 1, :] = fbuf[t, f, 129 - depth : 128, :]
            tbuf[SOUTH_CORNER + 3 * f : SOUTH_CORNER + 3 * f + depth - 1, :] = fbuf[t, f, 0 : depth - 1, :]
        acc = jnp.transpose(tbuf[...])
        for f in range(NF):
            v = fbuf[t, f]
            acc = jnp.where((lane >= 8 * f) & (lane < 8 * f + 8), lane_pick(v, edge_lane), acc)
        out_ref[pl.ds(t, N - SHIFT, stride=4), :] = acc[SHIFT:]
        out_ref[pl.ds(t + 4 * (N - SHIFT), SHIFT, stride=4), :] = acc[:SHIFT]

        @pl.when(t == 0)
        def _():
            fetch.wait()

        @pl.when(mig_ref[0, lax.axis_index("curve")] == t)
        def _():
            pltpu.make_async_copy(fbuf.at[t], leave_ref, lsem).start()

        return carry

    lax.fori_loop(0, 4, body, 0)
    pltpu.make_async_copy(fbuf.at[0], leave_ref, lsem).wait()


def make_messages(mig, fields, mask):
    return pl.pallas_call(
        message_kernel,
        out_shape=(
            jax.ShapeDtypeStruct((4 * N, N), F32),
            jax.ShapeDtypeStruct((NF, N, N), F32),
        ),
        in_specs=[pl.BlockSpec(memory_space=pl.ANY)] * 3,
        out_specs=(pl.BlockSpec(memory_space=pltpu.VMEM), pl.BlockSpec(memory_space=pl.ANY)),
        scratch_shapes=[
            pltpu.VMEM((4, NF, N, N), F32),
            pltpu.VMEM((4, N, N), jnp.int32),
            pltpu.VMEM((N, N), F32),
            pltpu.SMEM((1, N), jnp.int32),
            pltpu.SemaphoreType.DMA((4,)),
            pltpu.SemaphoreType.DMA((4,)),
            pltpu.SemaphoreType.DMA,
            pltpu.SemaphoreType.DMA,
        ],
        compiler_params=pltpu.CompilerParams(vmem_limit_bytes=VMEM_ALL),
        cost_estimate=pl.CostEstimate(flops=2_000_000, bytes_accessed=3_000_000, transcendentals=0),
        name="messages",
    )(mig, fields, mask)


def route_kernel(w_hbm, e_hbm, s_hbm, n_hbm, side_hbm, mig_hbm, rows_hbm, out_ref, w_ref, e_ref, s_ref, n_ref, side_ref, mig_ref, table, picked, sem, osem):
    fetches = tuple(
        pltpu.make_async_copy(a, b, sem.at[k])
        for k, (a, b) in enumerate(
            (
                (w_hbm, w_ref), (e_hbm, e_ref), (s_hbm, s_ref), (n_hbm, n_ref),
                (side_hbm, side_ref), (mig_hbm, mig_ref), (rows_hbm, table),
            )
        )
    )
    for cp in fetches:
        cp.start()
    position = (lax.axis_index("curve") + SHIFT) & (N - 1)
    lane = lanes_of((1, N))
    from_west = (lane < NORTH) & ((lane & 4) != 0)
    from_east = (lane < NORTH) & ((lane & 4) == 0)
    from_south = lane < SOUTH
    from_north = lane < NORTH_CORNER
    from_low = lane < SOUTH_CORNER
    for cp in fetches:
        cp.wait()

    def pick(p, place, corners):
        s, n = s_ref[p], n_ref[p]
        row = table[pl.ds(n, 1), :]
        if corners:
            far = jnp.where(from_low, table[pl.ds(side_ref[s], 1), :], table[pl.ds(side_ref[n], 1), :])
            row = jnp.where(from_north, row, far)
        row = jnp.where(from_south, table[pl.ds(s, 1), :], row)
        row = jnp.where(from_east, table[pl.ds(e_ref[p], 1), :], row)
        row = jnp.where(from_west, table[pl.ds(w_ref[p], 1), :], row)
        picked[pl.ds(place, 1), :] = row

    def put(c):
        span = pl.ds(N * c, N)
        return pltpu.make_async_copy(picked.at[span], out_ref.at[span], osem.at[c])

    def run(corners):
        def body(d, carry):
            moving = mig_ref[d]
            first = 4 * d
            for i in range(3):
                pick(jnp.where(moving <= i, first + (i + 1), first + i), first + i, corners)
            pick(first + moving, first + 7, corners)
            return carry

        def chunk(c, carry):
            def four(g, inner):
                for u in range(4):
                    body(32 * c + 4 * g + u, inner)
                return inner

            lax.fori_loop(0, 8, four, 0)
            put(c).start()
            return carry

        pick(4 * (N - 1) + mig_ref[N - 1], 3, corners)
        lax.fori_loop(0, 4, chunk, 0)

    at_corner = (position < CORNER) | (position >= N - CORNER)

    @pl.when(at_corner)
    def _():
        run(True)

    @pl.when(jnp.logical_not(at_corner))
    def _():
        run(False)

    for c in range(4):
        put(c).wait()


def route(tables, mig, rows):
    hbm = pl.BlockSpec(memory_space=pl.ANY)
    return pl.pallas_call(
        route_kernel,
        out_shape=jax.ShapeDtypeStruct((4 * N, N), F32),
        in_specs=[hbm] * 7,
        out_specs=hbm,
        scratch_shapes=[
            *(pltpu.SMEM((4 * N,), jnp.int32) for _ in range(5)),
            pltpu.SMEM((N,), jnp.int32),
            pltpu.VMEM((4 * N, N), F32),
            pltpu.VMEM((4 * N + SUB, N), F32),
            pltpu.SemaphoreType.DMA((7,)),
            pltpu.SemaphoreType.DMA((4,)),
        ],
        compiler_params=pltpu.CompilerParams(vmem_limit_bytes=VMEM_ALL),
        cost_estimate=pl.CostEstimate(flops=2_000_000, bytes_accessed=2_000_000, transcendentals=0),
        name="route",
    )(*tables, mig, rows)


def own_strips(patch, i, lane, cols, rows):
    at = lane - 32 * i
    inside = (at >= 4) & (at < 28)
    source = jnp.where(at < 16, at + 116, at - 20) & (N - 1)
    for f in range(NF):
        v = patch[f]
        cols[f] = jnp.where(inside, lane_pick(v, source), cols[f])
        rows[pl.ds((f * KR + 4) * SUB + 2 * i, 8, stride=SUB), :] = patch[f, 0:8, :]
        rows[pl.ds((f * KR) * SUB + 2 * i + 1, 8, stride=SUB), :] = patch[f, 120:128, :]


def interior(patch, work, terms):
    for f in range(NF):
        for j in range(JM):
            v = patch[f, pl.ds(j, SUB, stride=JM), :]
            if f == 5:
                v = TIME_STEP * v
                work[1, f, j] = v
            work[0, f, j] = v

    def step(k, carry):
        a, b = k & 1, 1 - (k & 1)

        def load(j, f):
            return work[a, f, j]

        def store(j, f, value):
            work[b, f, j] = value

        advance_tiles(load, store, terms, 0, JM, JM)
        return carry

    lax.fori_loop(0, 4, step, 0)
    for f in range(5):
        for j in range(JM):
            patch[f, pl.ds(j, SUB, stride=JM), :] = work[0, f, j]


def interior_kernel(arrival, refs):
    mig_hbm, fields_ref, mask_ref = refs[:3]
    if arrival:
        come_ref, cols_in, rows_in = refs[3:6]
        out_ref, cols_ref, rows_ref = refs[6:9]
    else:
        near_ref, leave_ref = refs[3:5]
        out_ref, cols_ref, rows_ref, passed_ref = refs[5:9]
        known_refs = refs[9:14]
        del leave_ref, passed_ref
    fbuf, mbuf, work, terms, cols, rows, mig_ref, near_buf, known, fsem, msem, csem, osem, gsem, ksem = refs[-15:]
    first = 2 if arrival else 0
    slots = 2 if arrival else 3
    come = slots

    def fetches(n):
        return (
            pltpu.make_async_copy(fields_ref.at[first + n], fbuf.at[n], fsem.at[n]),
            pltpu.make_async_copy(mask_ref.at[first + n], mbuf.at[n], msem.at[n]),
        )

    fetch_mig = pltpu.make_async_copy(mig_hbm, mig_ref, gsem.at[0])
    fetch_mig.start()
    for n in range(slots):
        for cp in fetches(n):
            cp.start()
    if arrival:
        given = (
            pltpu.make_async_copy(cols_in, cols, csem.at[0]),
            pltpu.make_async_copy(rows_in, rows, csem.at[1]),
            pltpu.make_async_copy(come_ref, fbuf.at[come], fsem.at[come]),
        )
        for cp in given:
            cp.start()
    else:
        fetch_near = pltpu.make_async_copy(near_ref, near_buf, gsem.at[1])
        fetch_near.start()
        cols[...] = jnp.zeros(cols.shape, F32)
        rows[...] = jnp.zeros(rows.shape, F32)
    fetch_mig.wait()
    moving = mig_ref[0, lax.axis_index("curve")]
    if not arrival:
        fetch_near.wait()
        for c in range(4):
            part = [jnp.maximum(near_buf[k : k + 1, c * N : (c + 1) * N], 0) for k in range(4)]
            part.append(jnp.where(((lax.axis_index("curve") + SHIFT) & (N - 1)) < N // 2, part[1], part[0]))
            for k in range(5):
                known[k, c : c + 1, :] = part[k]
        give = [pltpu.make_async_copy(known.at[k], known_refs[k], ksem.at[k]) for k in range(5)]
        for cp in give:
            cp.start()
    lane = lanes_of((N, N))

    def mask_patch(n):
        wet = mbuf[n].astype(F32)
        for f in range(4):
            fbuf[n, f] = fbuf[n, f] * wet

    def place_of(n):
        place = n + (moving <= first + n).astype(jnp.int32)
        return jnp.where(n == 1, come, place) if arrival else place

    def run(n, carry):
        place = place_of(n)

        @pl.when(n == 0)
        def _():
            for t in range(slots):
                for cp in fetches(t):
                    cp.wait()
            if arrival:
                for cp in given:
                    cp.wait()

        if arrival:

            @pl.when(n == 0)
            def _():
                mask_patch(place)
        else:
            mask_patch(place)
        patch = fbuf.at[place]
        own_strips(patch, first + n, lane, cols, rows)
        interior(patch, work, terms)
        pltpu.make_async_copy(patch, out_ref.at[n], osem.at[n]).start()
        return carry

    lax.fori_loop(0, 2, run, 0)
    last = (
        pltpu.make_async_copy(cols, cols_ref, csem.at[0]),
        pltpu.make_async_copy(rows, rows_ref, csem.at[1]),
    )
    for cp in last:
        cp.start()
    for n in range(2):
        pltpu.make_async_copy(fbuf.at[n], out_ref.at[n], osem.at[n]).wait()
    for cp in last:
        cp.wait()
    if not arrival:
        for cp in give:
            cp.wait()


def interiors(arrival, name, mig, fields, mask, *more):
    hbm = pl.BlockSpec(memory_space=pl.ANY)

    def kernel(*refs):
        interior_kernel(arrival, refs)

    return pl.pallas_call(
        kernel,
        out_shape=(
            jax.ShapeDtypeStruct((2, NF, N, N), F32),
            jax.ShapeDtypeStruct((NF, N, N), F32),
            jax.ShapeDtypeStruct((NF * KR * SUB, N), F32),
        )
        + (() if arrival else (jax.ShapeDtypeStruct((NF, N, N), F32),) + (jax.ShapeDtypeStruct((4, N), jnp.int32),) * 5),
        in_specs=[hbm] * (3 + len(more)),
        out_specs=(hbm,) * (3 if arrival else 9),
        input_output_aliases={} if arrival else {4: 3},
        scratch_shapes=[
            pltpu.VMEM((3, NF, N, N), F32),
            pltpu.VMEM((3, N, N), jnp.int32),
            pltpu.VMEM((2, NF, JM, SUB, N), F32),
            pltpu.VMEM((TERMS, JM, SUB, N), F32),
            pltpu.VMEM((NF, N, N), F32),
            pltpu.VMEM((NF * KR * SUB, N), F32),
            pltpu.SMEM((1, N), jnp.int32),
            pltpu.VMEM((4, 4 * N), jnp.int32),
            pltpu.VMEM((5, 4, N), jnp.int32),
            pltpu.SemaphoreType.DMA((3,)),
            pltpu.SemaphoreType.DMA((3,)),
            pltpu.SemaphoreType.DMA((2,)),
            pltpu.SemaphoreType.DMA((2,)),
            pltpu.SemaphoreType.DMA((2,)),
            pltpu.SemaphoreType.DMA((5,)),
        ],
        compiler_params=pltpu.CompilerParams(vmem_limit_bytes=VMEM_ALL),
        cost_estimate=pl.CostEstimate(flops=60_000_000, bytes_accessed=1_600_000, transcendentals=0),
        name=name,
    )(mig, fields, mask, *more)


def finish_kernel(
    near_hbm, mig_hbm, halo_hbm, cols_ref, rows_ref, low_ref, high_ref, out_ref,
    near_ref, mig_ref, halo_ref, wide, own, flip, cwork, rwork, terms, stage, isem, ssem, osem, nsem,
):
    turn = 4 * SHIFT
    fetch_halo = (
        pltpu.make_async_copy(halo_hbm.at[pl.ds(4 * N - turn, turn)], halo_ref.at[pl.ds(0, turn)], nsem.at[0]),
        pltpu.make_async_copy(halo_hbm.at[pl.ds(0, 4 * N - turn)], halo_ref.at[pl.ds(turn, 4 * N - turn)], nsem.at[3]),
    )
    fetch_near = pltpu.make_async_copy(near_hbm, near_ref, nsem.at[1])
    fetch_mig = pltpu.make_async_copy(mig_hbm, mig_ref, nsem.at[2])
    for cp in fetch_halo:
        cp.start()
    fetch_near.start()
    fetch_mig.start()
    fetch_cols = pltpu.make_async_copy(cols_ref, own, isem.at[0])
    fetch_rows = pltpu.make_async_copy(rows_ref, rwork.at[0], isem.at[1])
    fetch_cols.start()
    fetch_rows.start()
    fetch_low = pltpu.make_async_copy(low_ref, stage.at[0:2], ssem.at[0])
    fetch_high = pltpu.make_async_copy(high_ref, stage.at[2:4], ssem.at[1])
    fetch_low.start()
    fetch_high.start()
    lane_all = lanes_of((N, N))
    for cp in fetch_halo:
        cp.wait()

    def halo_columns(f, carry):
        inside = ((lane_all & 31) >= 12) & ((lane_all & 31) < 20)
        halo_lane = ((lane_all & 31) - 12 + 8 * f) & (N - 1)
        for i in range(4):
            moved = lane_pick(halo_ref[pl.ds(i, N, stride=4), :], halo_lane)
            acc = moved if i == 0 else jnp.where(lane_all >= 32 * i, moved, acc)
        wide[f, 4 : 4 + N, :] = jnp.where(inside, acc, own[f])
        return carry

    fetch_cols.wait()
    lax.fori_loop(0, NF, halo_columns, 0)
    fetch_rows.wait()

    lane4 = lanes_of((4, N))
    ends_lane = jnp.where((lane4 & 31) < 16, (lane4 & 31) - 12, (lane4 & 31) - 20) & (N - 1)
    flip[N:136, :] = jnp.zeros((8, N), F32)

    def halo_rows(i, carry):
        flip[0:N, :] = jnp.transpose(halo_ref[pl.ds(i, N, stride=4), :])
        here = lane4 // 32 == i
        for f in range(NF):
            for high in range(2):
                if high:
                    edge = flip[SOUTH + 4 * f : SOUTH + 4 * f + 4, :]
                    corner = flip[SOUTH_CORNER + 3 * f : SOUTH_CORNER + 3 * f + 4, :]
                else:
                    shift = 0 if f < 5 else 1
                    edge = flip[NORTH + 4 * f - shift : NORTH + 4 * f - shift + 4, :]
                    start = NORTH_CORNER - 1 + 3 * f if f < 5 else NORTH_CORNER + 13
                    corner = flip[start : start + 4, :]
                ends = jnp.where(
                    ((lane4 & 31) >= 12) & ((lane4 & 31) < 20), lane_pick(corner, ends_lane), lane_pick(edge, ends_lane)
                )
                at = 132 if high else 0
                wide[f, at : at + 4, :] = jnp.where(here, ends, wide[f, at : at + 4, :])
                k0 = 8 if high else 0
                for r in range(4):
                    rwork[0, f, k0 + r, pl.ds(2 * i + high, 1), :] = edge[r : r + 1, :]
        return carry

    lax.fori_loop(0, 4, halo_rows, 0)

    def arrange(f, carry):
        for j in range(JC):
            cwork[0, f, j] = wide[f, pl.ds(j, SUB, stride=JC), :]
        return carry

    lax.fori_loop(0, NF, arrange, 0)

    fetch_near.wait()
    fetch_mig.wait()
    dev = lax.axis_index("curve")
    moving = mig_ref[0, dev]
    before = (dev + N - 1) & (N - 1)
    lane = lanes_of((SUB, N))
    sub = subs_of((SUB, N))
    group = lane // 32

    lacks = []
    for i in range(4):
        patch = 4 * dev + slot_of(i, moving) if i < 3 else 4 * before + mig_ref[0, before]
        lacks.append([(near_ref[k, patch] < 0).astype(jnp.int32) for k in range(4)])

    def by_group(k):
        v = jnp.zeros((SUB, N), jnp.int32)
        for i in range(4):
            v = jnp.where(group == i, lacks[i][k], v)
        return v != 0

    in_group = lane & 31
    no_west, no_east, no_south, no_north = (by_group(k) for k in range(4))
    source = jnp.where(no_west & ((in_group == 18) | (in_group == 19)), lane - in_group + 20, lane)
    source = jnp.where(no_east & ((in_group == 12) | (in_group == 13)), lane - in_group + 11, source)
    low_fix = no_south & (sub == 0)
    high_fix = no_north & (sub == 7)
    row_flag = jnp.zeros((SUB, N), jnp.int32)
    for i in range(4):
        row_flag = jnp.where(sub == 2 * i, lacks[i][2], row_flag)
        row_flag = jnp.where(sub == 2 * i + 1, lacks[i][3], row_flag)
    row_low = (row_flag != 0) & ((sub & 1) == 0)
    row_high = (row_flag != 0) & ((sub & 1) == 1)

    def edge(f, carry):
        for j in range(JC):
            cwork[0, f, j] = lane_pick(cwork[0, f, j], source)
        for j in (2, 3):
            cwork[0, f, j] = jnp.where(low_fix, cwork[0, f, 4], cwork[0, f, j])
        for j in (13, 14):
            cwork[0, f, j] = jnp.where(high_fix, cwork[0, f, 12], cwork[0, f, j])
        return carry

    def step(k, carry):
        @pl.when(k == 0)
        def _():
            lax.fori_loop(0, NF, edge, 0)
            for j in range(JC):
                v = TIME_STEP * cwork[0, 5, j]
                cwork[0, 5, j] = v
                cwork[1, 5, j] = v

        @pl.when(k == 2)
        def _():
            lax.fori_loop(0, 5, edge, 0)

        a, b = k & 1, 1 - (k & 1)

        def load(j, f):
            return cwork[a, f, j]

        def store(j, f, value):
            cwork[b, f, j] = value

        advance_tiles(load, store, terms, 0, JC, JC)
        return carry

    lax.fori_loop(0, 4, step, 0)

    def row_edges(fields):
        for f in fields:
            for k in (2, 3):
                rwork[0, f, k] = jnp.where(row_low, rwork[0, f, 4], rwork[0, f, k])
            for k in (8, 9):
                rwork[0, f, k] = jnp.where(row_high, rwork[0, f, 7], rwork[0, f, k])

    row_edges((5,))
    for j in range(KR):
        v = TIME_STEP * rwork[0, 5, j]
        rwork[0, 5, j] = v
        rwork[1, 5, j] = v

    def row_step(k, carry):
        @pl.when((k & 1) == 0)
        def _():
            row_edges(range(5))

        a, b = k & 1, 1 - (k & 1)

        def load(j, f):
            return rwork[a, f, j]

        def store(j, f, value):
            rwork[b, f, j] = value

        @pl.when(k < 2)
        def _():
            advance_tiles(load, store, terms, 1, 11, KR)

        @pl.when(k >= 2)
        def _():
            advance_tiles(load, store, terms, 3, 9, KR)

        return carry

    lax.fori_loop(0, 4, row_step, 0)

    def restore(f, carry):
        for j in range(JC):
            wide[f, pl.ds(j, SUB, stride=JC), :] = cwork[0, f, j]
        return carry

    lax.fori_loop(0, 5, restore, 0)
    fetch_low.wait()
    fetch_high.wait()

    def slot(i):
        return jnp.where(i == 3, moving, i + (moving <= i).astype(jnp.int32))

    def merge(i, carry):
        at = slot(i)
        strip_lane = (jnp.where(lane_all < 64, lane_all + 20, lane_all - 116) + 32 * i) & (N - 1)
        pltpu.make_async_copy(stage.at[i, 5], out_ref.at[at, 5], osem.at[i]).start()
        for f in range(5):
            for r in range(4):
                stage[i, f, r : r + 1, :] = rwork[0, f, 4 + r, pl.ds(2 * i, 1), :]
                stage[i, f, 124 + r : 125 + r, :] = rwork[0, f, 4 + r, pl.ds(2 * i + 1, 1), :]
            strip = wide[f, 4 : 4 + N, :]
            stage[i, f] = jnp.where((lane_all < 4) | (lane_all >= 124), lane_pick(strip, strip_lane), stage[i, f])
            pltpu.make_async_copy(stage.at[i, f], out_ref.at[at, f], osem.at[i]).start()
        return carry

    lax.fori_loop(0, 4, merge, 0)
    for i in range(4):
        pltpu.make_async_copy(stage.at[i], out_ref.at[slot(i)], osem.at[i]).wait()


def finish(near, mig, halo, cols, rows, low, high):
    hbm = pl.BlockSpec(memory_space=pl.ANY)
    return pl.pallas_call(
        finish_kernel,
        out_shape=jax.ShapeDtypeStruct((4, NF, N, N), F32),
        in_specs=[hbm] * 7,
        out_specs=hbm,
        scratch_shapes=[
            pltpu.SMEM((4, 4 * N), jnp.int32),
            pltpu.SMEM((1, N), jnp.int32),
            pltpu.VMEM((4 * N, N), F32),
            pltpu.VMEM((NF, 136, N), F32),
            pltpu.VMEM((NF, N, N), F32),
            pltpu.VMEM((136, N), F32),
            pltpu.VMEM((2, NF, JC, SUB, N), F32),
            pltpu.VMEM((2, NF, KR, SUB, N), F32),
            pltpu.VMEM((TERMS, JC, SUB, N), F32),
            pltpu.VMEM((4, NF, N, N), F32),
            pltpu.SemaphoreType.DMA((2,)),
            pltpu.SemaphoreType.DMA((2,)),
            pltpu.SemaphoreType.DMA((4,)),
            pltpu.SemaphoreType.DMA((4,)),
        ],
        compiler_params=pltpu.CompilerParams(vmem_limit_bytes=VMEM_ALL),
        cost_estimate=pl.CostEstimate(flops=30_000_000, bytes_accessed=3_000_000, transcendentals=0),
        name="finish",
    )(near, mig, halo, cols, rows, low, high)


def swap(rows):
    return lax.all_to_all(rows.reshape(N, 4, N), "curve", 0, 0, tiled=True).reshape(4 * N, N)


def shards(fields, wet_mask, neighbors, migration):
    near, mig = neighbors.T, migration.T
    owners = lax.axis_size("curve")
    messages, leaving = make_messages(mig, fields, wet_mask)
    spread = swap(messages)
    low, cols, rows, leaving, *tables = interiors(False, "first", mig, fields, wet_mask, near, leaving)
    patch = lax.ppermute(leaving, "curve", [(d, (d + 1) % owners) for d in range(owners)])
    tables = [table.reshape(4 * N) for table in tables]
    halo = swap(route(tables, migration.reshape(N), spread))
    high, cols, rows = interiors(True, "second", mig, fields, wet_mask, patch, cols, rows)
    return finish(near, mig, halo, cols, rows.reshape(NF, KR, SUB, N), low, high)


def solution(mesh):
    placed = (P("curve", None, None, None), P("curve", None, None), P(), P())
    return jax.shard_map(
        shards, mesh=mesh, in_specs=placed, out_specs=P("curve", None, None, None), check_vma=False
    )
```

```python
import jax
import jax.numpy as jnp
from jax import lax
from jax.experimental import pallas as pl
from jax.experimental.pallas import tpu as pltpu
from jax.sharding import PartitionSpec as P

GRAVITY = 9.81
TIME_STEP = 0.04
DRY_EPS = 0.01
CAPACITY = 0.02
EROSION = 0.5
SETTLING = 0.2
POROSITY = 0.4

F32 = jnp.float32
NF = 6
N = 128
SUB = 8
JM = 16
JC = 17
KR = 12
VMEM_ALL = 67_043_328
SHIFT = 16
CORNER = 3

NORTH, SOUTH, NORTH_CORNER, SOUTH_CORNER = 48, 71, 94, 111


def lanes_of(shape):
    return lax.broadcasted_iota(jnp.int32, shape, 1)


def subs_of(shape):
    return lax.broadcasted_iota(jnp.int32, shape, 0)


def lane_pick(v, index):
    return jnp.take_along_axis(v, index, axis=1, mode="promise_in_bounds")


def to_the_east(v):
    return pltpu.roll(v, N - 1, 1)


def to_the_west(v):
    return pltpu.roll(v, 1, 1)


def root(x):
    return x * lax.rsqrt(x)


def root_from_zero(x):
    return root(jnp.maximum(x, 1e-30))


def celerity_term(h):
    return jnp.maximum((0.5 * GRAVITY) * h, 1e-30)


def cell_terms(h, qx, qy, m):
    hp = jnp.maximum(h, 0.0)
    h2 = h * h
    a = h / (h2 + DRY_EPS)
    u, v, s = qx * a, qy * a, m * a
    r = root(hp + 0.01)
    half = (0.5 * GRAVITY) * h2
    hg = celerity_term(h)
    return dict(
        h=h, hg=hg, qx=qx, qy=qy, m=m, r=r, ru=r * u, rv=r * v, rs=r * s,
        fxx=qx * u + half, fxy=qx * v, fyy=qy * v + half, fxs=qx * s, fys=qy * s,
    )


ROLLED_X = ("h", "qx", "qy", "m", "r", "ru", "rv", "rs", "fxx", "fxy", "fxs")


def face_twice(L, R, along_x):
    qn, qt, rn, rt, fn, fs = (
        ("qx", "qy", "ru", "rv", "fxx", "fxs") if along_x else ("qy", "qx", "rv", "ru", "fyy", "fys")
    )
    c = root(L["hg"] + R["hg"]) + 0.1
    iw, ic2 = 1.0 / (L["r"] + R["r"]), 1.0 / (c + c)
    U = (L[rn] + R[rn]) * iw
    W = (L[rt] + R[rt]) * iw
    S = (L["rs"] + R["rs"]) * iw
    dh = R["h"] - L["h"]
    dn = R[qn] - L[qn]
    dt = R[qt] - L[qt]
    dm = R["m"] - L["m"]
    up, um = U + c, U - c
    p1 = jnp.abs(um) * ((up * dh - dn) * ic2)
    p3 = jnp.abs(up) * ((dn - um * dh) * ic2)
    mid = jnp.abs(U)
    b = p1 + p3
    f_h = (L[qn] + R[qn]) - b
    f_n = (L[fn] + R[fn]) - (p1 * um + p3 * up)
    e = b - mid * dh
    f_t = (L["fxy"] + R["fxy"]) - (W * e + mid * dt)
    f_s = (L[fs] + R[fs]) - (S * e + mid * dm)
    return f_h, f_n, f_t, f_s


def update(C, bed, bed_e, bed_w, bed_n, bed_s, fric, dx, fyn, fys):
    k = 0.5 * TIME_STEP
    h = C["h"]
    slope = (TIME_STEP * GRAVITY * 0.5) * h
    nh = h - k * (dx[0] + (fyn[0] - fys[0]))
    nx = C["qx"] - k * (dx[1] + (fyn[2] - fys[2])) - slope * (bed_e - bed_w)
    ny = C["qy"] - k * (dx[2] + (fyn[1] - fys[1])) - slope * (bed_n - bed_s)
    nm = C["m"] - k * (dx[3] + (fyn[3] - fys[3]))
    a = nh / (nh * nh + DRY_EPS)
    vx, vy = nx * a, ny * a
    speed2 = vx * vx + vy * vy
    speed = root_from_zero(speed2)
    depth = jnp.maximum(nh, 0.0) + 0.1
    factor = depth / (depth + fric * speed)
    conc = nm * a
    gain = jnp.maximum((TIME_STEP * EROSION * CAPACITY) * speed2 - (TIME_STEP * EROSION) * conc, 0.0)
    gain = gain - (TIME_STEP * SETTLING) * conc
    nm = nm + gain
    nb = bed - (1.0 / (1.0 - POROSITY)) * gain
    return nh, nx * factor, ny * factor, nm, nb


KEPT = ("hg", "r", "ru", "rv", "rs", "fxy", "fyy", "fys", "fxx", "fxs")
FLUX = len(KEPT)
MOVED = FLUX + 4
TERMS = MOVED + len(ROLLED_X)


def x_terms(load, terms, j, faces):
    cur = cell_terms(*(load(j, f) for f in range(4)))
    for n, key in enumerate(KEPT):
        terms[n, j] = cur[key]
    if faces:
        for n, key in enumerate(ROLLED_X):
            terms[MOVED + n, j] = to_the_east(cur[key])


def x_faces(load, terms, j):
    L = {key: load(j, f) for f, key in enumerate(("h", "qx", "qy", "m"))}
    for n, key in enumerate(KEPT):
        L[key] = terms[n, j]
    R = {key: terms[MOVED + n, j] for n, key in enumerate(ROLLED_X)}
    R["hg"] = celerity_term(R["h"])
    east = face_twice(L, R, True)
    for n in range(4):
        terms[FLUX + n, j] = east[n]


def y_pass(load, store, terms, lo, hi, last):
    wraps = lo == 0

    def around(j, get):
        if j < 0:
            return pltpu.roll(get(last - 1), 1, 0)
        if j == last:
            return pltpu.roll(get(0), SUB - 1, 0)
        return get(j)

    def cell(j):
        C = {key: around(j, lambda t: load(t, f)) for f, key in enumerate(("h", "qx", "qy", "m"))}
        for n, key in enumerate(KEPT):
            C[key] = around(j, lambda t: terms[n, t])
        return C

    if wraps:
        top = face_twice(cell(last - 1), cell(last), False)
        south = tuple(pltpu.roll(x, 1, 0) for x in top)
    else:
        south = face_twice(cell(lo - 1), cell(lo), False)
    cur = cell(lo)
    for j in range(lo, hi):
        if wraps and j == last - 1:
            nxt, north = None, top
        else:
            nxt = cell(j + 1)
            north = face_twice(cur, nxt, False)
        bed = load(j, 4)
        dx = tuple(terms[FLUX + n, j] - to_the_west(terms[FLUX + n, j]) for n in range(4))
        bed_n, bed_s = (around(t, lambda t: load(t, 4)) for t in (j + 1, j - 1))
        new = update(
            cur, bed, to_the_east(bed), to_the_west(bed), bed_n, bed_s, load(j, 5), dx, north, south,
        )
        for f in range(5):
            store(j, f, new[f])
        south = north
        cur = cell(j + 1) if j + 1 < hi else None


def advance_tiles(load, store, terms, lo, hi, last):
    span = range(last) if lo == 0 else range(lo - 1, hi + 1)
    for j in span:
        x_terms(load, terms, j, lo <= j < hi)
    for j in range(lo, hi):
        x_faces(load, terms, j)
    y_pass(load, store, terms, lo, hi, last)


def slot_of(i, moving):
    if i == 3:
        return moving
    return i + (moving <= i).astype(jnp.int32)


def message_kernel(mig_hbm, fields_ref, mask_ref, out_ref, leave_ref, fbuf, mbuf, tbuf, mig_ref, fsem, msem, gsem, lsem):
    def fetches(t):
        return (
            pltpu.make_async_copy(fields_ref.at[t], fbuf.at[t], fsem.at[t]),
            pltpu.make_async_copy(mask_ref.at[t], mbuf.at[t], msem.at[t]),
        )

    for t in range(4):
        for cp in fetches(t):
            cp.start()
    fetch = pltpu.make_async_copy(mig_hbm, mig_ref, gsem)
    fetch.start()
    lane = lanes_of((N, N))
    edge_lane = (lane & 3) + jnp.where((lane & 4) != 0, 124, 0)

    def body(t, carry):
        for cp in fetches(t):
            cp.wait()
        wet = mbuf[t].astype(F32)
        for f in range(4):
            fbuf[t, f] = fbuf[t, f] * wet
        for f in range(NF):
            depth = 4 if f < 5 else 3
            low = 4 - depth
            tbuf[NORTH + 4 * f : NORTH + 4 * f + depth, :] = fbuf[t, f, 124 + low : 128, :]
            tbuf[SOUTH + 4 * f : SOUTH + 4 * f + depth, :] = fbuf[t, f, 0:depth, :]
            tbuf[NORTH_CORNER + 3 * f : NORTH_CORNER + 3 * f + depth - 1, :] = fbuf[t, f, 129 - depth : 128, :]
            tbuf[SOUTH_CORNER + 3 * f : SOUTH_CORNER + 3 * f + depth - 1, :] = fbuf[t, f, 0 : depth - 1, :]
        acc = jnp.transpose(tbuf[...])
        for f in range(NF):
            v = fbuf[t, f]
            acc = jnp.where((lane >= 8 * f) & (lane < 8 * f + 8), lane_pick(v, edge_lane), acc)
        out_ref[pl.ds(t, N - SHIFT, stride=4), :] = acc[SHIFT:]
        out_ref[pl.ds(t + 4 * (N - SHIFT), SHIFT, stride=4), :] = acc[:SHIFT]

        @pl.when(t == 0)
        def _():
            fetch.wait()

        @pl.when(mig_ref[0, lax.axis_index("curve")] == t)
        def _():
            pltpu.make_async_copy(fbuf.at[t], leave_ref, lsem).start()

        return carry

    lax.fori_loop(0, 4, body, 0)
    pltpu.make_async_copy(fbuf.at[0], leave_ref, lsem).wait()


def make_messages(mig, fields, mask):
    return pl.pallas_call(
        message_kernel,
        out_shape=(
            jax.ShapeDtypeStruct((4 * N, N), F32),
            jax.ShapeDtypeStruct((NF, N, N), F32),
        ),
        in_specs=[pl.BlockSpec(memory_space=pl.ANY)] * 3,
        out_specs=(pl.BlockSpec(memory_space=pltpu.VMEM), pl.BlockSpec(memory_space=pl.ANY)),
        scratch_shapes=[
            pltpu.VMEM((4, NF, N, N), F32),
            pltpu.VMEM((4, N, N), jnp.int32),
            pltpu.VMEM((N, N), F32),
            pltpu.SMEM((1, N), jnp.int32),
            pltpu.SemaphoreType.DMA((4,)),
            pltpu.SemaphoreType.DMA((4,)),
            pltpu.SemaphoreType.DMA,
            pltpu.SemaphoreType.DMA,
        ],
        compiler_params=pltpu.CompilerParams(vmem_limit_bytes=VMEM_ALL),
        cost_estimate=pl.CostEstimate(flops=2_000_000, bytes_accessed=3_000_000, transcendentals=0),
        name="messages",
    )(mig, fields, mask)


def route_kernel(w_hbm, e_hbm, s_hbm, n_hbm, side_hbm, mig_hbm, rows_hbm, out_ref, w_ref, e_ref, s_ref, n_ref, side_ref, mig_ref, table, picked, sem, osem):
    fetches = tuple(
        pltpu.make_async_copy(a, b, sem.at[k])
        for k, (a, b) in enumerate(
            (
                (rows_hbm, table), (w_hbm, w_ref), (e_hbm, e_ref), (s_hbm, s_ref), (n_hbm, n_ref),
                (side_hbm, side_ref), (mig_hbm, mig_ref),
            )
        )
    )
    for cp in fetches:
        cp.start()
    position = (lax.axis_index("curve") + SHIFT) & (N - 1)
    lane = lanes_of((1, N))
    from_west = (lane < NORTH) & ((lane & 4) != 0)
    from_east = (lane < NORTH) & ((lane & 4) == 0)
    from_south = lane < SOUTH
    from_north = lane < NORTH_CORNER
    from_low = lane < SOUTH_CORNER
    for cp in fetches:
        cp.wait()

    def pick(p, place, corners):
        s, n = s_ref[p], n_ref[p]
        row = table[pl.ds(n, 1), :]
        if corners:
            far = jnp.where(from_low, table[pl.ds(side_ref[s], 1), :], table[pl.ds(side_ref[n], 1), :])
            row = jnp.where(from_north, row, far)
        row = jnp.where(from_south, table[pl.ds(s, 1), :], row)
        row = jnp.where(from_east, table[pl.ds(e_ref[p], 1), :], row)
        row = jnp.where(from_west, table[pl.ds(w_ref[p], 1), :], row)
        picked[pl.ds(place, 1), :] = row

    def put(c):
        span = pl.ds(N * c, N)
        return pltpu.make_async_copy(picked.at[span], out_ref.at[span], osem.at[c])

    def run(corners):
        def body(d, carry):
            moving = mig_ref[d]
            first = 4 * d
            for i in range(3):
                pick(jnp.where(moving <= i, first + (i + 1), first + i), first + i, corners)
            pick(first + moving, first + 7, corners)
            return carry

        def chunk(c, carry):
            def eight(g, inner):
                for u in range(8):
                    body(32 * c + 8 * g + u, inner)
                return inner

            lax.fori_loop(0, 4, eight, 0)
            put(c).start()
            return carry

        pick(4 * (N - 1) + mig_ref[N - 1], 3, corners)
        lax.fori_loop(0, 4, chunk, 0)

    at_corner = (position < CORNER) | (position >= N - CORNER)

    @pl.when(at_corner)
    def _():
        run(True)

    @pl.when(jnp.logical_not(at_corner))
    def _():
        run(False)

    for c in range(4):
        put(c).wait()


def route(tables, mig, rows):
    hbm = pl.BlockSpec(memory_space=pl.ANY)
    return pl.pallas_call(
        route_kernel,
        out_shape=jax.ShapeDtypeStruct((4 * N, N), F32),
        in_specs=[hbm] * 7,
        out_specs=hbm,
        scratch_shapes=[
            *(pltpu.SMEM((4 * N,), jnp.int32) for _ in range(5)),
            pltpu.SMEM((N,), jnp.int32),
            pltpu.VMEM((4 * N, N), F32),
            pltpu.VMEM((4 * N + SUB, N), F32),
            pltpu.SemaphoreType.DMA((7,)),
            pltpu.SemaphoreType.DMA((4,)),
        ],
        compiler_params=pltpu.CompilerParams(vmem_limit_bytes=VMEM_ALL),
        cost_estimate=pl.CostEstimate(flops=2_000_000, bytes_accessed=2_000_000, transcendentals=0),
        name="route",
    )(*tables, mig, rows)


def own_strips(patch, i, lane, cols, rows):
    at = lane - 32 * i
    inside = (at >= 4) & (at < 28)
    source = jnp.where(at < 16, at + 116, at - 20) & (N - 1)
    for f in range(NF):
        v = patch[f]
        cols[f] = jnp.where(inside, lane_pick(v, source), cols[f])
        rows[pl.ds((f * KR + 4) * SUB + 2 * i, 8, stride=SUB), :] = patch[f, 0:8, :]
        rows[pl.ds((f * KR) * SUB + 2 * i + 1, 8, stride=SUB), :] = patch[f, 120:128, :]


def interior(patch, work, terms):
    for f in range(NF):
        for j in range(JM):
            v = patch[f, pl.ds(j, SUB, stride=JM), :]
            if f == 5:
                v = TIME_STEP * v
                work[1, f, j] = v
            work[0, f, j] = v

    def step(k, carry):
        a, b = k & 1, 1 - (k & 1)

        def load(j, f):
            return work[a, f, j]

        def store(j, f, value):
            work[b, f, j] = value

        advance_tiles(load, store, terms, 0, JM, JM)
        return carry

    lax.fori_loop(0, 4, step, 0)
    for f in range(5):
        for j in range(JM):
            patch[f, pl.ds(j, SUB, stride=JM), :] = work[0, f, j]


def interior_kernel(arrival, refs):
    mig_hbm, fields_ref, mask_ref = refs[:3]
    if arrival:
        come_ref, cols_in, rows_in = refs[3:6]
        out_ref, cols_ref, rows_ref = refs[6:9]
    else:
        near_ref, leave_ref = refs[3:5]
        out_ref, cols_ref, rows_ref, passed_ref = refs[5:9]
        known_refs = refs[9:14]
        del leave_ref, passed_ref
    fbuf, mbuf, work, terms, cols, rows, mig_ref, near_buf, known, fsem, msem, csem, osem, gsem, ksem = refs[-15:]
    first = 2 if arrival else 0
    slots = 2 if arrival else 3
    come = slots

    def fetches(n):
        return (
            pltpu.make_async_copy(fields_ref.at[first + n], fbuf.at[n], fsem.at[n]),
            pltpu.make_async_copy(mask_ref.at[first + n], mbuf.at[n], msem.at[n]),
        )

    fetch_mig = pltpu.make_async_copy(mig_hbm, mig_ref, gsem.at[0])
    fetch_mig.start()
    for n in range(slots):
        for cp in fetches(n):
            cp.start()
    if arrival:
        given = (
            pltpu.make_async_copy(cols_in, cols, csem.at[0]),
            pltpu.make_async_copy(rows_in, rows, csem.at[1]),
            pltpu.make_async_copy(come_ref, fbuf.at[come], fsem.at[come]),
        )
        for cp in given:
            cp.start()
    else:
        fetch_near = pltpu.make_async_copy(near_ref, near_buf, gsem.at[1])
        fetch_near.start()
        cols[...] = jnp.zeros(cols.shape, F32)
        rows[...] = jnp.zeros(rows.shape, F32)
    fetch_mig.wait()
    moving = mig_ref[0, lax.axis_index("curve")]
    if not arrival:
        fetch_near.wait()
        for c in range(4):
            part = [jnp.maximum(near_buf[k : k + 1, c * N : (c + 1) * N], 0) for k in range(4)]
            part.append(jnp.where(((lax.axis_index("curve") + SHIFT) & (N - 1)) < N // 2, part[1], part[0]))
            for k in range(5):
                known[k, c : c + 1, :] = part[k]
        give = [pltpu.make_async_copy(known.at[k], known_refs[k], ksem.at[k]) for k in range(5)]
        for cp in give:
            cp.start()
    lane = lanes_of((N, N))

    def mask_patch(n):
        wet = mbuf[n].astype(F32)
        for f in range(4):
            fbuf[n, f] = fbuf[n, f] * wet

    def place_of(n):
        place = n + (moving <= first + n).astype(jnp.int32)
        return jnp.where(n == 1, come, place) if arrival else place

    def run(n, carry):
        place = place_of(n)

        @pl.when(n == 0)
        def _():
            for t in range(slots):
                for cp in fetches(t):
                    cp.wait()
            if arrival:
                for cp in given:
                    cp.wait()

        if arrival:

            @pl.when(n == 0)
            def _():
                mask_patch(place)
        else:
            mask_patch(place)
        patch = fbuf.at[place]
        own_strips(patch, first + n, lane, cols, rows)
        interior(patch, work, terms)
        pltpu.make_async_copy(patch, out_ref.at[n], osem.at[n]).start()
        return carry

    lax.fori_loop(0, 2, run, 0)
    last = (
        pltpu.make_async_copy(cols, cols_ref, csem.at[0]),
        pltpu.make_async_copy(rows, rows_ref, csem.at[1]),
    )
    for cp in last:
        cp.start()
    for n in range(2):
        pltpu.make_async_copy(fbuf.at[n], out_ref.at[n], osem.at[n]).wait()
    for cp in last:
        cp.wait()
    if not arrival:
        for cp in give:
            cp.wait()


def interiors(arrival, name, mig, fields, mask, *more):
    hbm = pl.BlockSpec(memory_space=pl.ANY)

    def kernel(*refs):
        interior_kernel(arrival, refs)

    return pl.pallas_call(
        kernel,
        out_shape=(
            jax.ShapeDtypeStruct((2, NF, N, N), F32),
            jax.ShapeDtypeStruct((NF, N, N), F32),
            jax.ShapeDtypeStruct((NF * KR * SUB, N), F32),
        )
        + (() if arrival else (jax.ShapeDtypeStruct((NF, N, N), F32),) + (jax.ShapeDtypeStruct((4, N), jnp.int32),) * 5),
        in_specs=[hbm] * (3 + len(more)),
        out_specs=(hbm,) * (3 if arrival else 9),
        input_output_aliases={} if arrival else {4: 3},
        scratch_shapes=[
            pltpu.VMEM((3, NF, N, N), F32),
            pltpu.VMEM((3, N, N), jnp.int32),
            pltpu.VMEM((2, NF, JM, SUB, N), F32),
            pltpu.VMEM((TERMS, JM, SUB, N), F32),
            pltpu.VMEM((NF, N, N), F32),
            pltpu.VMEM((NF * KR * SUB, N), F32),
            pltpu.SMEM((1, N), jnp.int32),
            pltpu.VMEM((4, 4 * N), jnp.int32),
            pltpu.VMEM((5, 4, N), jnp.int32),
            pltpu.SemaphoreType.DMA((3,)),
            pltpu.SemaphoreType.DMA((3,)),
            pltpu.SemaphoreType.DMA((2,)),
            pltpu.SemaphoreType.DMA((2,)),
            pltpu.SemaphoreType.DMA((2,)),
            pltpu.SemaphoreType.DMA((5,)),
        ],
        compiler_params=pltpu.CompilerParams(vmem_limit_bytes=VMEM_ALL),
        cost_estimate=pl.CostEstimate(flops=60_000_000, bytes_accessed=1_600_000, transcendentals=0),
        name=name,
    )(mig, fields, mask, *more)


def finish_kernel(
    near_hbm, mig_hbm, halo_hbm, cols_ref, rows_ref, low_ref, high_ref, out_ref,
    near_ref, mig_ref, halo_ref, wide, own, flip, cwork, rwork, terms, stage, isem, ssem, osem, nsem,
):
    turn = 4 * SHIFT
    fetch_halo = (
        pltpu.make_async_copy(halo_hbm.at[pl.ds(4 * N - turn, turn)], halo_ref.at[pl.ds(0, turn)], nsem.at[0]),
        pltpu.make_async_copy(halo_hbm.at[pl.ds(0, 4 * N - turn)], halo_ref.at[pl.ds(turn, 4 * N - turn)], nsem.at[3]),
    )
    fetch_near = pltpu.make_async_copy(near_hbm, near_ref, nsem.at[1])
    fetch_mig = pltpu.make_async_copy(mig_hbm, mig_ref, nsem.at[2])
    for cp in fetch_halo:
        cp.start()
    fetch_near.start()
    fetch_mig.start()
    fetch_cols = pltpu.make_async_copy(cols_ref, own, isem.at[0])
    fetch_rows = pltpu.make_async_copy(rows_ref, rwork.at[0], isem.at[1])
    fetch_cols.start()
    fetch_rows.start()
    fetch_low = pltpu.make_async_copy(low_ref, stage.at[0:2], ssem.at[0])
    fetch_high = pltpu.make_async_copy(high_ref, stage.at[2:4], ssem.at[1])
    lane_all = lanes_of((N, N))
    for cp in fetch_halo:
        cp.wait()

    def halo_columns(f, carry):
        inside = ((lane_all & 31) >= 12) & ((lane_all & 31) < 20)
        halo_lane = ((lane_all & 31) - 12 + 8 * f) & (N - 1)
        for i in range(4):
            moved = lane_pick(halo_ref[pl.ds(i, N, stride=4), :], halo_lane)
            acc = moved if i == 0 else jnp.where(lane_all >= 32 * i, moved, acc)
        wide[f, 4 : 4 + N, :] = jnp.where(inside, acc, own[f])
        return carry

    fetch_cols.wait()
    lax.fori_loop(0, NF, halo_columns, 0)
    fetch_rows.wait()
    fetch_low.start()
    fetch_high.start()

    lane4 = lanes_of((4, N))
    ends_lane = jnp.where((lane4 & 31) < 16, (lane4 & 31) - 12, (lane4 & 31) - 20) & (N - 1)
    flip[N:136, :] = jnp.zeros((8, N), F32)

    def halo_rows(i, carry):
        flip[0:N, :] = jnp.transpose(halo_ref[pl.ds(i, N, stride=4), :])
        here = lane4 // 32 == i
        for f in range(NF):
            for high in range(2):
                if high:
                    edge = flip[SOUTH + 4 * f : SOUTH + 4 * f + 4, :]
                    corner = flip[SOUTH_CORNER + 3 * f : SOUTH_CORNER + 3 * f + 4, :]
                else:
                    shift = 0 if f < 5 else 1
                    edge = flip[NORTH + 4 * f - shift : NORTH + 4 * f - shift + 4, :]
                    start = NORTH_CORNER - 1 + 3 * f if f < 5 else NORTH_CORNER + 13
                    corner = flip[start : start + 4, :]
                ends = jnp.where(
                    ((lane4 & 31) >= 12) & ((lane4 & 31) < 20), lane_pick(corner, ends_lane), lane_pick(edge, ends_lane)
                )
                at = 132 if high else 0
                wide[f, at : at + 4, :] = jnp.where(here, ends, wide[f, at : at + 4, :])
                k0 = 8 if high else 0
                for r in range(4):
                    rwork[0, f, k0 + r, pl.ds(2 * i + high, 1), :] = edge[r : r + 1, :]
        return carry

    lax.fori_loop(0, 4, halo_rows, 0)

    def arrange(f, carry):
        for j in range(JC):
            cwork[0, f, j] = wide[f, pl.ds(j, SUB, stride=JC), :]
        return carry

    lax.fori_loop(0, NF, arrange, 0)

    fetch_near.wait()
    fetch_mig.wait()
    dev = lax.axis_index("curve")
    moving = mig_ref[0, dev]
    before = (dev + N - 1) & (N - 1)
    lane = lanes_of((SUB, N))
    sub = subs_of((SUB, N))
    group = lane // 32

    lacks = []
    for i in range(4):
        patch = 4 * dev + slot_of(i, moving) if i < 3 else 4 * before + mig_ref[0, before]
        lacks.append([(near_ref[k, patch] < 0).astype(jnp.int32) for k in range(4)])

    def by_group(k):
        v = jnp.zeros((SUB, N), jnp.int32)
        for i in range(4):
            v = jnp.where(group == i, lacks[i][k], v)
        return v != 0

    in_group = lane & 31
    no_west, no_east, no_south, no_north = (by_group(k) for k in range(4))
    source = jnp.where(no_west & ((in_group == 18) | (in_group == 19)), lane - in_group + 20, lane)
    source = jnp.where(no_east & ((in_group == 12) | (in_group == 13)), lane - in_group + 11, source)
    low_fix = no_south & (sub == 0)
    high_fix = no_north & (sub == 7)
    row_flag = jnp.zeros((SUB, N), jnp.int32)
    for i in range(4):
        row_flag = jnp.where(sub == 2 * i, lacks[i][2], row_flag)
        row_flag = jnp.where(sub == 2 * i + 1, lacks[i][3], row_flag)
    row_low = (row_flag != 0) & ((sub & 1) == 0)
    row_high = (row_flag != 0) & ((sub & 1) == 1)

    def edge(f, carry):
        for j in range(JC):
            cwork[0, f, j] = lane_pick(cwork[0, f, j], source)
        for j in (2, 3):
            cwork[0, f, j] = jnp.where(low_fix, cwork[0, f, 4], cwork[0, f, j])
        for j in (13, 14):
            cwork[0, f, j] = jnp.where(high_fix, cwork[0, f, 12], cwork[0, f, j])
        return carry

    def step(k, carry):
        @pl.when(k == 0)
        def _():
            lax.fori_loop(0, NF, edge, 0)
            for j in range(JC):
                v = TIME_STEP * cwork[0, 5, j]
                cwork[0, 5, j] = v
                cwork[1, 5, j] = v

        @pl.when(k == 2)
        def _():
            lax.fori_loop(0, 5, edge, 0)

        a, b = k & 1, 1 - (k & 1)

        def load(j, f):
            return cwork[a, f, j]

        def store(j, f, value):
            cwork[b, f, j] = value

        advance_tiles(load, store, terms, 0, JC, JC)
        return carry

    lax.fori_loop(0, 4, step, 0)

    def row_edges(fields):
        for f in fields:
            for k in (2, 3):
                rwork[0, f, k] = jnp.where(row_low, rwork[0, f, 4], rwork[0, f, k])
            for k in (8, 9):
                rwork[0, f, k] = jnp.where(row_high, rwork[0, f, 7], rwork[0, f, k])

    row_edges((5,))
    for j in range(KR):
        v = TIME_STEP * rwork[0, 5, j]
        rwork[0, 5, j] = v
        rwork[1, 5, j] = v

    def row_step(k, carry):
        @pl.when((k & 1) == 0)
        def _():
            row_edges(range(5))

        a, b = k & 1, 1 - (k & 1)

        def load(j, f):
            return rwork[a, f, j]

        def store(j, f, value):
            rwork[b, f, j] = value

        @pl.when(k < 2)
        def _():
            advance_tiles(load, store, terms, 1, 11, KR)

        @pl.when(k >= 2)
        def _():
            advance_tiles(load, store, terms, 3, 9, KR)

        return carry

    lax.fori_loop(0, 4, row_step, 0)

    def restore(f, carry):
        for j in range(JC):
            wide[f, pl.ds(j, SUB, stride=JC), :] = cwork[0, f, j]
        return carry

    lax.fori_loop(0, 5, restore, 0)
    fetch_low.wait()
    fetch_high.wait()

    def slot(i):
        return jnp.where(i == 3, moving, i + (moving <= i).astype(jnp.int32))

    def merge(i, carry):
        at = slot(i)
        strip_lane = (jnp.where(lane_all < 64, lane_all + 20, lane_all - 116) + 32 * i) & (N - 1)
        pltpu.make_async_copy(stage.at[i, 5], out_ref.at[at, 5], osem.at[i]).start()
        for f in range(5):
            for r in range(4):
                stage[i, f, r : r + 1, :] = rwork[0, f, 4 + r, pl.ds(2 * i, 1), :]
                stage[i, f, 124 + r : 125 + r, :] = rwork[0, f, 4 + r, pl.ds(2 * i + 1, 1), :]
            strip = wide[f, 4 : 4 + N, :]
            stage[i, f] = jnp.where((lane_all < 4) | (lane_all >= 124), lane_pick(strip, strip_lane), stage[i, f])
            pltpu.make_async_copy(stage.at[i, f], out_ref.at[at, f], osem.at[i]).start()
        return carry

    lax.fori_loop(0, 4, merge, 0)
    for i in range(4):
        pltpu.make_async_copy(stage.at[i], out_ref.at[slot(i)], osem.at[i]).wait()


def finish(near, mig, halo, cols, rows, low, high):
    hbm = pl.BlockSpec(memory_space=pl.ANY)
    return pl.pallas_call(
        finish_kernel,
        out_shape=jax.ShapeDtypeStruct((4, NF, N, N), F32),
        in_specs=[hbm] * 7,
        out_specs=hbm,
        scratch_shapes=[
            pltpu.SMEM((4, 4 * N), jnp.int32),
            pltpu.SMEM((1, N), jnp.int32),
            pltpu.VMEM((4 * N, N), F32),
            pltpu.VMEM((NF, 136, N), F32),
            pltpu.VMEM((NF, N, N), F32),
            pltpu.VMEM((136, N), F32),
            pltpu.VMEM((2, NF, JC, SUB, N), F32),
            pltpu.VMEM((2, NF, KR, SUB, N), F32),
            pltpu.VMEM((TERMS, JC, SUB, N), F32),
            pltpu.VMEM((4, NF, N, N), F32),
            pltpu.SemaphoreType.DMA((2,)),
            pltpu.SemaphoreType.DMA((2,)),
            pltpu.SemaphoreType.DMA((4,)),
            pltpu.SemaphoreType.DMA((4,)),
        ],
        compiler_params=pltpu.CompilerParams(vmem_limit_bytes=VMEM_ALL),
        cost_estimate=pl.CostEstimate(flops=30_000_000, bytes_accessed=3_000_000, transcendentals=0),
        name="finish",
    )(near, mig, halo, cols, rows, low, high)


def swap(rows):
    return lax.all_to_all(rows.reshape(N, 4, N), "curve", 0, 0, tiled=True).reshape(4 * N, N)


def shards(fields, wet_mask, neighbors, migration):
    near, mig = neighbors.T, migration.T
    owners = lax.axis_size("curve")
    messages, leaving = make_messages(mig, fields, wet_mask)
    spread = swap(messages)
    low, cols, rows, leaving, *tables = interiors(False, "first", mig, fields, wet_mask, near, leaving)
    patch = lax.ppermute(leaving, "curve", [(d, (d + 1) % owners) for d in range(owners)])
    tables = [table.reshape(4 * N) for table in tables]
    halo = swap(route(tables, migration.reshape(N), spread))
    high, cols, rows = interiors(True, "second", mig, fields, wet_mask, patch, cols, rows)
    return finish(near, mig, halo, cols, rows.reshape(NF, KR, SUB, N), low, high)


def solution(mesh):
    placed = (P("curve", None, None, None), P("curve", None, None), P(), P())
    return jax.shard_map(
        shards, mesh=mesh, in_specs=placed, out_specs=P("curve", None, None, None), check_vma=False
    )
```
